256 devices in a mesh: row: 8 (over x, z_hi), col: 32 (over z_lo, y, core).
Axes of the slice: x: 4, y: 4, z: 8 (z_hi: 2, z_lo: 4; z = z_hi * 4 + z_lo), core: 2. Of those that a mesh axis runs over, the one named last changes fastest.
Arguments:
- pair: float32 [1024, 1024, 128], P('row', 'col'), may hold values from -6 to 6
- single: float32 [1024, 384], P(('row', 'col')), may hold values from -6 to 6
- target_bins: int32 [1024, 1024], P('row', 'col'), may hold values from 0 to 63
- token_pad: int32 [1024], P(('row', 'col')), may hold values from 0 to 1, as said below
- w_gate: float32 [128, 512], replicated, may hold values from -0.5 to 0.5
- w_up: float32 [128, 512], replicated, may hold values from -0.5 to 0.5
- w_out: float32 [512, 128], replicated, may hold values from -0.25 to 0.25
- w_bias: float32 [128, 16], replicated, may hold values from -25 to 25
- w_query: float32 [384, 384], replicated, may hold values from -0.3125 to 0.3125
- w_key: float32 [384, 384], replicated, may hold values from -0.3125 to 0.3125
- w_value: float32 [384, 384], replicated, may hold values from -0.3125 to 0.3125
- w_gating: float32 [384, 384], replicated, may hold values from -0.3125 to 0.3125
- w_attn_out: float32 [384, 384], replicated, may hold values from -0.3125 to 0.3125
- w_dist: float32 [128, 64], replicated, may hold values from -12 to 12
- b_dist: float32 [64], replicated, may hold values from -2 to 2
Outputs:
- pair_out: float32 [1024, 1024, 128], P('row', 'col')
- single_out: float32 [1024, 384], P(('row', 'col'))
The draws below stay inside these ranges and needn't reach their ends.
Inputs may be any that keep to these rules, and one draw needn't show every extreme that they name: `token_pad`: 1 for the first tokens and 0 for the rest, with at least 512 ones.
All inputs are finite; a program needn't handle non-finite values.
Results may differ from the reference program's by a relative error of at most 0.0003.
Values sent between devices are 32-bit elements; how exact they have to be, the bound alone decides.
No kernel may reach another device: no remote copies, remote signals or barrier semaphores. Data moves between devices by JAX's collectives and lax.ppermute only.
A program may use at most 64 MiB of HBM per device.

```python
from functools import partial
import jax
import jax.numpy as jnp
from jax import lax

PAIR = 128
TRANS = 512
SINGLE = 384
HEADS = 16
HEAD_DIM = 24
BINS = 64
TOK_DEV = 4
N = 1024
N_COL = 32


def draw_token_pad(key, part):
    length = jax.random.randint(jax.random.fold_in(key, 11), (), N // 2, N + 1)
    return (jnp.arange(N, dtype=jnp.int32) < length).astype(jnp.int32)


def draw_w_bias(key, part):
    base = jnp.clip(jax.random.normal(jax.random.fold_in(key, 23), (PAIR, HEADS), jnp.float32), -4.0, 4.0) * PAIR ** (-0.5)
    return base


def draw_w_dist(key, part):
    base = jnp.clip(jax.random.normal(jax.random.fold_in(key, 31), (PAIR, BINS), jnp.float32), -4.0, 4.0) * 0.25
    return base


def touch_ends(values, stream_key, low, largest):
    index_at = [jax.random.randint(jax.random.fold_in(stream_key, axis), (), 0, length) for axis, length in enumerate(values.shape)]
    longest = values.shape.index(max(values.shape))
    next_to = index_at[:longest] + [(index_at[longest] + 1) % values.shape[longest]] + index_at[longest + 1:]
    return values.at[tuple(index_at)].set(low).at[tuple(next_to)].set(largest)


def block_scale(rng, extent, shards, least, high):
    def one(dim, parts):
        steps = jax.random.uniform(jax.random.fold_in(jax.random.fold_in(rng, 6), dim), (parts,), jnp.float32, least / len(shards), high / len(shards))
        return jnp.repeat(jnp.exp(steps), extent[dim] // parts).reshape((-1,) + (1,) * (len(extent) - dim - 1))

    gain = one(*shards[0])
    for cut in shards[1:]:
        gain = gain * one(*cut)
    return gain


def scatter_about(stream_key, shape, spread, bound, pieces=(), held_as=jnp.bfloat16):
    loudness = block_scale(stream_key, shape, pieces, -0.22, 0.18) if pieces else 1.0
    values = jax.random.normal(stream_key, shape, jnp.float32) * spread * loudness
    return jnp.minimum(jnp.maximum(values, -bound), bound).astype(held_as)


def setup_inputs(seed: int = 0) -> dict:
    seeds = jax.random.split(jax.random.key(seed), 16)
    return {
        "pair": scatter_about(seeds[0], (N, N, PAIR), 1.0, 6.0, ((0, 8), (1, 32)), jnp.float32),
        "single": scatter_about(seeds[1], (N, SINGLE), 1.0, 6.0, ((0, 256),), jnp.float32),
        "target_bins": touch_ends(jax.random.randint(seeds[2], (N, N), 0, BINS), jax.random.fold_in(seeds[2], 1), 0, BINS - 1).astype(jnp.int32),
        "token_pad": draw_token_pad(jax.random.fold_in(seeds[15], 71), 0),
        "w_gate": scatter_about(seeds[4], (PAIR, TRANS), PAIR ** -0.5, 0.5, (), jnp.float32),
        "w_up": scatter_about(seeds[5], (PAIR, TRANS), PAIR ** -0.5, 0.5, (), jnp.float32),
        "w_out": scatter_about(seeds[6], (TRANS, PAIR), TRANS ** -0.5, 0.25, (), jnp.float32),
        "w_bias": draw_w_bias(jax.random.fold_in(seeds[15], 71), 0),
        "w_query": scatter_about(seeds[8], (SINGLE, SINGLE), SINGLE ** -0.5, 0.3125, (), jnp.float32),
        "w_key": scatter_about(seeds[9], (SINGLE, SINGLE), SINGLE ** -0.5, 0.3125, (), jnp.float32),
        "w_value": scatter_about(seeds[10], (SINGLE, SINGLE), SINGLE ** -0.5, 0.3125, (), jnp.float32),
        "w_gating": scatter_about(seeds[11], (SINGLE, SINGLE), SINGLE ** -0.5, 0.3125, (), jnp.float32),
        "w_attn_out": scatter_about(seeds[12], (SINGLE, SINGLE), SINGLE ** -0.5, 0.3125, (), jnp.float32),
        "w_dist": draw_w_dist(jax.random.fold_in(seeds[15], 71), 0),
        "b_dist": jnp.clip(jax.random.uniform(seeds[14], (BINS,), jnp.float32, -2.0, 2.0), -2.0, 2.0),
    }


HI = lax.Precision.HIGHEST

def layer_norm(x):
    mean = lax.optimization_barrier(jnp.mean(x, axis=-1, keepdims=True))
    centred = x - mean
    var = lax.optimization_barrier(jnp.mean(centred * centred, axis=-1, keepdims=True))
    return centred * lax.rsqrt(var + 1e-05)

def dense(x, w):
    flat = x.reshape(-1, x.shape[-1])
    out = jnp.dot(flat, w, precision=HI, preferred_element_type=jnp.float32)
    return out.reshape(x.shape[:-1] + (w.shape[1],))

def transition_rows(block, w_gate, w_up, w_out, w_bias):
    normed = layer_norm(block)
    hidden = jax.nn.silu(dense(normed, w_gate)) * dense(normed, w_up)
    mid = block + dense(hidden, w_out)
    bias = dense(layer_norm(mid), w_bias)
    return (mid, bias)

def dist_rows(start, mid, target_bins, pad_float, w_dist, b_dist, block):
    mid_rows = lax.dynamic_slice_in_dim(mid, start, block, 0)
    mid_cols = lax.dynamic_slice_in_dim(mid, start, block, 1)
    proj_rows = dense(mid_rows, w_dist)
    proj_cols = jnp.transpose(dense(mid_cols, w_dist), (1, 0, 2))
    logits = proj_rows + proj_cols + b_dist
    shifted = logits - lax.optimization_barrier(jnp.max(logits, axis=-1, keepdims=True))
    expo = jnp.exp(shifted)
    probs = expo / lax.optimization_barrier(jnp.sum(expo, axis=-1, keepdims=True))
    pad_rows = lax.dynamic_slice_in_dim(pad_float, start, block, 0)
    mask = pad_rows[:, None] * pad_float[None, :]
    bin_ids = jnp.arange(w_dist.shape[1], dtype=jnp.int32)
    t_rows = lax.dynamic_slice_in_dim(target_bins, start, block, 0)
    t_cols = jnp.transpose(lax.dynamic_slice_in_dim(target_bins, start, block, 1))
    onehot = (t_rows[:, :, None] == bin_ids).astype(jnp.float32)
    onehot_flip = (t_cols[:, :, None] == bin_ids).astype(jnp.float32)
    delta = mask[:, :, None] * (2.0 * probs - onehot - onehot_flip)
    return mid_rows + dense(delta, jnp.transpose(w_dist))

def reference(pair, single, target_bins, token_pad, w_gate, w_up, w_out, w_bias, w_query, w_key, w_value, w_gating, w_attn_out, w_dist, b_dist):
    block = TOK_DEV * N_COL // 4
    count = N // block
    blocks = pair.reshape(count, block, N, PAIR)
    mid, bias = lax.map(partial(transition_rows, w_gate=w_gate, w_up=w_up, w_out=w_out, w_bias=w_bias), blocks)
    mid = mid.reshape(N, N, PAIR)
    bias = bias.reshape(N, N, HEADS)
    single_norm = layer_norm(single)
    query = dense(single_norm, w_query).reshape(N, HEADS, HEAD_DIM)
    key = dense(single_norm, w_key).reshape(N, HEADS, HEAD_DIM)
    value = dense(single_norm, w_value).reshape(N, HEADS, HEAD_DIM)
    gating = jax.nn.sigmoid(dense(single_norm, w_gating))
    scores = jnp.einsum('ihd,jhd->ijh', query, key, precision=HI) / jnp.sqrt(jnp.float32(HEAD_DIM)) + bias
    scores = jnp.where((token_pad > 0)[None, :, None], scores, jnp.float32(-1000000000.0))
    top = lax.optimization_barrier(jnp.max(scores, axis=1, keepdims=True))
    expo = jnp.exp(scores - top)
    total = lax.optimization_barrier(jnp.sum(expo, axis=1))
    attended = jnp.einsum('ijh,jhd->ihd', expo, value, precision=HI) / total[:, :, None]
    single_out = single + dense(gating * attended.reshape(N, SINGLE), w_attn_out)
    pad_float = token_pad.astype(jnp.float32)
    starts = (jnp.arange(count) * block).astype(jnp.int32)
    pair_out = lax.map(partial(dist_rows, mid=mid, target_bins=target_bins, pad_float=pad_float, w_dist=w_dist, b_dist=b_dist, block=block), starts)
    pair_out = pair_out.reshape(N, N, PAIR)
    return (pair_out, single_out)
```

```python
import jax
import jax.numpy as jnp
from jax import lax
from jax.experimental import pallas as pl
from jax.experimental.pallas import tpu as pltpu
from jax.sharding import Mesh, PartitionSpec as P

F32 = jnp.float32
BF16 = jnp.bfloat16
ALL = ("x", "zh", "zl", "yh", "yl", "core")
COL = ("zl", "yh", "yl", "core")
PLANE = ("x", "yh", "yl", "core")
SIZES = (4, 2, 4, 2, 2, 2)


def flat_index(coords):
    index = 0
    for c, n in zip(coords, SIZES):
        index = index * n + c
    return index


def all_coords():
    out = [()]
    for n in SIZES:
        out = [c + (k,) for c in out for k in range(n)]
    return out


def halves(x):
    hi = x.astype(BF16)
    lo = (x - hi.astype(F32)).astype(BF16)
    return hi, lo


def mm(a, b):
    return jnp.dot(a, b, preferred_element_type=F32)


def mm_nt(a, b):
    return lax.dot_general(a, b, (((1,), (1,)), ((), ())), preferred_element_type=F32)


def mm3(a, b, dot=mm):
    ah, al = halves(a)
    bh, bl = halves(b)
    return dot(ah, bh) + (dot(al, bh) + dot(ah, bl))


def norm(x):
    mean = jnp.mean(x, axis=-1, keepdims=True)
    centred = x - mean
    var = jnp.mean(centred * centred, axis=-1, keepdims=True)
    return centred * lax.rsqrt(var + 1e-05)


def lanes_of(shape):
    return lax.broadcasted_iota(jnp.int32, shape, len(shape) - 1)


def doubled_projection(wdt_ref):
    d = wdt_ref[...]
    d = d - d[0:1, :]
    z = jnp.zeros_like(d)
    both = jnp.concatenate(
        [jnp.concatenate([d, z], axis=1), jnp.concatenate([z, d], axis=1)], axis=0
    )
    hi, lo = halves(both.T)
    return jnp.concatenate([hi, lo], axis=1)


def project(a, b, wp_ref):
    xh, xl = halves(jnp.concatenate([a, b], axis=1))
    p = mm(xh, wp_ref[...])
    return p[:, :128] + (p[:, 128:] + mm(xl, wp_ref[:, :128]))


def transition_kernel(
    pair_ref, tt_ref, wg_ref, wu_ref, wo_ref, wdt_ref, mid_ref, proj_ref, w1_ref, w2_ref, wp_ref
):
    step = pl.program_id(0)

    @pl.when(step == 0)
    def _():
        for k, ref in enumerate((wg_ref, wu_ref)):
            hi, lo = halves(ref[...])
            w1_ref[k, 0] = jnp.concatenate([hi, hi], axis=0)
            w1_ref[k, 1] = jnp.concatenate([lo, lo], axis=0)
        hi, lo = halves(wo_ref[...])
        w2_ref[...] = jnp.concatenate([hi, lo], axis=1)
        wp_ref[...] = doubled_projection(wdt_ref)

    x = pair_ref[...].reshape(512, 128)
    nh, nl = halves(norm(x))
    both = jnp.concatenate([nh, nl], axis=1)
    out = jnp.zeros((512, 128), F32)
    for c in range(0, 512, 256):
        gate = mm(both, w1_ref[0, 0, :, c : c + 256]) + mm(both, w1_ref[0, 1, :, c : c + 256])
        up = mm(both, w1_ref[1, 0, :, c : c + 256]) + mm(both, w1_ref[1, 1, :, c : c + 256])
        hidden = gate / (1.0 + jnp.exp(-gate)) * up
        hh, hl = halves(hidden)
        o = mm(hh, w2_ref[c : c + 256, :])
        out = out + (o[:, :128] + (o[:, 128:] + mm(hl, w2_ref[c : c + 256, :128])))
    mid = x + out
    mid_ref[...] = mid.reshape(4, 1, 4, 32, 128)
    split = mid.reshape(16, 2, 16, 128)
    proj = project(split[:, 0].reshape(256, 128), split[:, 1].reshape(256, 128), wp_ref)
    turned = pltpu.roll(tt_ref[...].astype(F32), (128 - 4 * step) % 128, 1)
    lane = lanes_of((16, 128))
    for k in range(4):
        for w in range(4):
            i = k * 32 + w
            a = turned[0:16, i : i + 1]
            b = turned[16:32, i : i + 1]
            mark = jnp.where(lane == 0, a, jnp.where(lane == 64, b, 0.0))
            n = (k * 4 + w) * 16
            proj_ref[0, k, w] = proj[n : n + 16] + mark


def own_kernel(mid_ref, wdt_ref, bd_ref, wb_ref, own_ref, bias_ref, wp_ref, w3_ref, n_ref):
    @pl.when(pl.program_id(0) == 0)
    def _():
        wp_ref[...] = doubled_projection(wdt_ref)
        w = wb_ref[...]
        lane = lanes_of((128, 128))
        for k in range(8):
            hi, lo = halves(jnp.where(lane // 16 == k, w, 0.0))
            row = jnp.concatenate([hi, lo], axis=1)
            w3_ref[k] = jnp.concatenate([row, row], axis=0)

    own = project(mid_ref[0:512], mid_ref[512:1024], wp_ref)
    own_ref[...] = (own + bd_ref[...]).reshape(16, 32, 128)
    n_ref[...] = norm(mid_ref[...])
    acc = jnp.zeros((128, 256), F32)
    for k in range(8):
        x = jnp.concatenate(
            [n_ref[pl.ds(g * 8 + k, 32, stride=32), :] for g in range(4)], axis=0
        )
        hi, lo = halves(x)
        acc = acc + mm(jnp.concatenate([hi, lo], axis=1), w3_ref[k])
    acc = acc[:, :128] + acc[:, 128:]
    for g in range(4):
        bias_ref[:, g * 128 : (g + 1) * 128] = acc[g * 32 : (g + 1) * 32]


def attention_kernel(
    xr_ref, xc_ref, bias_ref, wq_ref, wk_ref, wv_ref, msg_ref, rowpad_ref, colpad_ref
):
    def tokens(ref, n):
        x = jnp.concatenate([ref[pl.ds(q, n, stride=4), :] for q in range(3)], axis=1)
        return norm(x), ref[pl.ds(3, n, stride=4), :][:, 0:1]

    rows, row_pad = tokens(xr_ref, 128)
    cols, col_pad = tokens(xc_ref, 32)
    lane = lanes_of((16, 128))
    for m in range(4):
        a = row_pad[m * 32 : m * 32 + 16]
        b = row_pad[m * 32 + 16 : m * 32 + 32]
        rowpad_ref[m * 16 : (m + 1) * 16, :] = jnp.where(lane < 64, a, b)
    colpad_ref[...] = jnp.broadcast_to(col_pad, (32, 128))
    query = mm3(rows, wq_ref[...]) * (24.0**-0.5)
    key = mm3(cols, wk_ref[...])
    value = mm3(cols, wv_ref[...])
    of_head = lanes_of((16, 384)) // 24 == lax.broadcasted_iota(jnp.int32, (16, 384), 0)

    def spread(y):
        return jnp.where(of_head[None], y[:, None, :], 0.0).reshape(512, 384)

    scores = mm3(query, spread(key), mm_nt) + bias_ref[...]
    of_key = lanes_of((32, 512)) // 16 == lax.broadcasted_iota(jnp.int32, (32, 512), 0)
    pad_lane = jnp.sum(jnp.where(of_key, col_pad, 0.0), axis=0, keepdims=True)
    scores = jnp.where(pad_lane > 0.5, scores, -1000000000.0)

    def over_keys(y, op):
        r = op(op(y[:, :128], y[:, 128:256]), op(y[:, 256:384], y[:, 384:]))
        for shift in (16, 32, 64):
            r = op(r, pltpu.roll(r, shift, 1))
        return r

    top = over_keys(scores, jnp.maximum)
    expo = jnp.exp(scores - jnp.concatenate([top] * 4, axis=1))
    total = over_keys(expo, jnp.add)
    acc = mm3(expo, spread(value))
    lane = lanes_of((128, 128))
    tail = jnp.where(lane < 16, total, jnp.where(lane < 32, top, 0.0))
    for q in range(3):
        msg_ref[pl.ds(q, 128, stride=4), :] = acc[:, q * 128 : (q + 1) * 128]
    msg_ref[pl.ds(3, 128, stride=4), :] = tail


def merge_kernel(msg_ref, single_ref, wg_ref, wo_ref, out_ref):
    lane = lanes_of((32, 128))
    accs, factors, totals = [], [], []
    for t in range(4):
        part = [msg_ref[pl.ds(4 * t + q, 32, stride=16), :] for q in range(4)]
        accs.append(jnp.concatenate(part[:3], axis=1))
        tail = part[3]
        local = pltpu.roll(tail, 112, 1)
        top = jnp.max(local, axis=0, keepdims=True)
        f = jnp.where(lane < 16, jnp.exp(local - top), 0.0)
        factors.append(f)
        totals.append(jnp.sum(f * tail, axis=0, keepdims=True))
    expand = jnp.where(
        lanes_of((128, 384)) // 24 == lax.broadcasted_iota(jnp.int32, (128, 384), 0), 1.0, 0.0
    )
    stacked = jnp.concatenate(factors + totals + totals, axis=0)
    wide = jnp.dot(stacked, expand, precision=lax.Precision.HIGHEST, preferred_element_type=F32)
    rows = []
    for t in range(4):
        num = jnp.sum(wide[t * 32 : (t + 1) * 32] * accs[t], axis=0, keepdims=True)
        rows.append(num / wide[128 + t : 129 + t])
    attended = jnp.concatenate(rows, axis=0)
    single = single_ref[...]
    g = mm3(norm(single), wg_ref[...])
    out_ref[...] = single + mm3(attended / (1.0 + jnp.exp(-g)), wo_ref[...])


def gradient_kernel(
    place_ref, *refs
):
    parts = refs[:8]
    own_ref, mid_ref, tt_ref, rowpad_ref, colpad_ref, wdt_ref, out_ref, f_ref, w_ref, d_ref = refs[8:]
    m = pl.program_id(0)

    @pl.when(m == 0)
    def _():
        d = wdt_ref[...]
        z = jnp.zeros_like(d)
        both = jnp.concatenate(
            [jnp.concatenate([d, z], axis=1), jnp.concatenate([z, d], axis=1)], axis=0
        )
        hi, lo = halves(both)
        w_ref[0] = jnp.concatenate([hi, hi], axis=0)
        w_ref[1] = jnp.concatenate([lo, lo], axis=0)

    for p in range(8):
        f_ref[pl.ds(pl.multiple_of(place_ref[p] * 64, 64), 64), :] = parts[p][0]
    lane = lanes_of((32, 128))
    first = lane < 64
    bins = lane % 64
    bin_float = bins.astype(F32)
    turned = pltpu.roll(tt_ref[...].astype(F32), (128 - 32 * m) % 128, 1)
    col_pad = colpad_ref[...]

    def seg(op, y, fill):
        a = op(jnp.where(first, y, fill), axis=-1, keepdims=True)
        b = op(jnp.where(first, fill, y), axis=-1, keepdims=True)
        return jnp.where(first, a, b)

    for i in range(16):
        flip = f_ref[pl.ds(i, 32, stride=16), :]
        t_flip = jnp.where(first, flip[:, 0:1], flip[:, 64:65])
        t_own = jnp.where(first, turned[:, i : i + 1], turned[:, 16 + i : 17 + i])
        logits = own_ref[i] + jnp.where(bins == 0, 0.0, flip)
        expo = jnp.exp(logits - seg(jnp.max, logits, -3.0e38))
        probs2 = expo * (2.0 / seg(jnp.sum, expo, 0.0))
        hits = jnp.where(bin_float == t_flip, 1.0, 0.0) + jnp.where(bin_float == t_own, 1.0, 0.0)
        mask = col_pad * rowpad_ref[i : i + 1, :]
        hi, lo = halves(mask * (probs2 - hits))
        d_ref[i * 32 : (i + 1) * 32, :] = jnp.concatenate([hi, lo], axis=1)
    change = mm(d_ref[...], w_ref[0]) + mm(d_ref[...], w_ref[1])
    out_ref[0:16] = mid_ref[0:16] + change[:, :128].reshape(16, 32, 128)
    out_ref[16:32] = mid_ref[16:32] + change[:, 128:].reshape(16, 32, 128)


def full(shape):
    return pl.BlockSpec(shape, lambda *_: (0,) * len(shape))


def struct(*shape):
    return jax.ShapeDtypeStruct(shape, F32)


def per_device(
    pair,
    single,
    target_bins,
    token_pad,
    w_gate,
    w_up,
    w_out,
    w_bias,
    w_query,
    w_key,
    w_value,
    w_gating,
    w_attn_out,
    w_dist,
    b_dist,
):
    at = {name: lax.axis_index(name) for name in ALL}
    coords = all_coords()
    tt = target_bins.T
    wdt = w_dist.T

    tok = jnp.concatenate(
        [single, token_pad.astype(F32)[:, None], jnp.zeros((4, 127), F32)], axis=1
    ).reshape(16, 128)
    rows_tok = lax.all_to_all(
        jnp.broadcast_to(tok, (32, 16, 128)), COL, split_axis=0, concat_axis=0, tiled=True
    ).reshape(512, 128)

    mid, proj = pl.pallas_call(
        transition_kernel,
        grid=(8,),
        in_specs=[
            pl.BlockSpec((4, 1, 4, 32, 128), lambda s: (0, s, 0, 0, 0)),
            full((32, 128)),
            full((128, 512)),
            full((128, 512)),
            full((512, 128)),
            full((64, 128)),
        ],
        out_specs=[
            pl.BlockSpec((4, 1, 4, 32, 128), lambda s: (0, s, 0, 0, 0)),
            pl.BlockSpec((1, 4, 4, 16, 128), lambda s: (s, 0, 0, 0, 0)),
        ],
        out_shape=[struct(4, 8, 4, 32, 128), struct(8, 4, 4, 16, 128)],
        scratch_shapes=[
            pltpu.VMEM((2, 2, 256, 512), BF16),
            pltpu.VMEM((512, 256), BF16),
            pltpu.VMEM((256, 256), BF16),
        ],
        name="transition",
    )(pair.reshape(4, 8, 4, 32, 128), tt, w_gate, w_up, w_out, wdt)

    spread = lax.all_to_all(
        proj.reshape(32, 64, 128), PLANE, split_axis=0, concat_axis=0, tiled=True
    ).reshape(8, 4, 64, 128)

    quarter = lax.dynamic_slice_in_dim(rows_tok, (at["yl"] * 2 + at["core"]) * 128, 128, 0)
    perm = [(flat_index(c), flat_index((c[2], c[3], c[0], c[1], c[4], c[5]))) for c in coords]
    cols_tok = lax.ppermute(quarter, ALL, perm)

    own, bias = pl.pallas_call(
        own_kernel,
        grid=(4,),
        in_specs=[
            pl.BlockSpec((1024, 128), lambda m: (m, 0)),
            full((64, 128)),
            full((1, 128)),
            full((128, 128)),
        ],
        out_specs=[
            pl.BlockSpec((16, 32, 128), lambda m: (m, 0, 0)),
            pl.BlockSpec((32, 512), lambda m: (m, 0)),
        ],
        out_shape=[struct(64, 32, 128), struct(128, 512)],
        scratch_shapes=[
            pltpu.VMEM((256, 256), BF16),
            pltpu.VMEM((8, 256, 256), BF16),
            pltpu.VMEM((1024, 128), F32),
        ],
        name="own",
    )(
        mid.reshape(4096, 128),
        wdt,
        jnp.tile(b_dist - b_dist[0], 2)[None],
        jnp.tile(w_bias, (1, 8)),
    )

    msg, rowpad, colpad = pl.pallas_call(
        attention_kernel,
        out_shape=[struct(512, 128), struct(64, 128), struct(32, 128)],
        name="attention",
    )(rows_tok, cols_tok, bias, w_query, w_key, w_value)

    parts, places = [], []
    for u in range(4):
        for v in range(2):
            piece = lax.dynamic_index_in_dim(
                spread, (at["x"] ^ u) * 2 + (at["yh"] ^ v), 0, keepdims=False
            )
            perm = [
                (flat_index(c), flat_index((c[2], c[3] ^ v, c[0] ^ u, c[1], c[4], c[5])))
                for c in coords
            ]
            parts.append(lax.ppermute(piece, ALL, perm))
            places.append((at["zl"] ^ u) * 2 + (at["zh"] ^ v))
    places = jnp.stack(places).astype(jnp.int32)

    merged = lax.all_to_all(
        msg.reshape(32, 16, 128), COL, split_axis=0, concat_axis=0, tiled=True
    ).reshape(512, 128)
    single_out = pl.pallas_call(
        merge_kernel, out_shape=struct(4, 384), name="merge"
    )(merged, single, w_gating, w_attn_out)

    pair_out = pl.pallas_call(
        gradient_kernel,
        grid_spec=pltpu.PrefetchScalarGridSpec(
            num_scalar_prefetch=1,
            grid=(4,),
            in_specs=[pl.BlockSpec((1, 64, 128), lambda m, _: (m, 0, 0))] * 8
            + [
                pl.BlockSpec((16, 32, 128), lambda m, _: (m, 0, 0)),
                pl.BlockSpec((32, 32, 128), lambda m, _: (m, 0, 0)),
                full((32, 128)),
                pl.BlockSpec((16, 128), lambda m, _: (m, 0)),
                full((32, 128)),
                full((64, 128)),
            ],
            out_specs=pl.BlockSpec((32, 32, 128), lambda m, _: (m, 0, 0)),
            scratch_shapes=[
                pltpu.VMEM((512, 128), F32),
                pltpu.VMEM((2, 256, 256), BF16),
                pltpu.VMEM((512, 256), BF16),
            ],
        ),
        out_shape=struct(128, 32, 128),
        name="gradient",
    )(places, *parts, own, mid.reshape(128, 32, 128), tt, rowpad, colpad, wdt)
    return (pair_out, single_out)


def solution(mesh):
    fine = Mesh(mesh.devices.reshape(SIZES), ALL)
    row, col = ("x", "zh"), COL
    in_specs = (
        P(row, col, None),
        P(ALL, None),
        P(row, col),
        P(ALL),
    ) + (P(),) * 11
    out_specs = (P(row, col, None), P(ALL, None))
    return jax.shard_map(
        per_device, mesh=fine, in_specs=in_specs, out_specs=out_specs, check_vma=False
    )
```

```python
import jax
import jax.numpy as jnp
from jax import lax
from jax.experimental import pallas as pl
from jax.experimental.pallas import tpu as pltpu
from jax.sharding import Mesh, PartitionSpec as P


F32 = jnp.float32
BF16 = jnp.bfloat16
ALL = ("x", "zh", "zl", "yh", "yl", "core")
COL = ("zl", "yh", "yl", "core")
PLANE = ("x", "yh", "yl", "core")
SIZES = (4, 2, 4, 2, 2, 2)


def flat_index(coords):
    index = 0
    for c, n in zip(coords, SIZES):
        index = index * n + c
    return index


def all_coords():
    out = [()]
    for n in SIZES:
        out = [c + (k,) for c in out for k in range(n)]
    return out


def halves(x):
    hi = x.astype(BF16)
    lo = (x - hi.astype(F32)).astype(BF16)
    return hi, lo


def mm(a, b):
    return jnp.dot(a, b, preferred_element_type=F32)


def mm_nt(a, b):
    return lax.dot_general(a, b, (((1,), (1,)), ((), ())), preferred_element_type=F32)


def mm3(a, b, dot=mm):
    ah, al = halves(a)
    bh, bl = halves(b)
    return dot(ah, bh) + (dot(al, bh) + dot(ah, bl))


def norm(x):
    mean = jnp.mean(x, axis=-1, keepdims=True)
    centred = x - mean
    var = jnp.mean(centred * centred, axis=-1, keepdims=True)
    return centred * lax.rsqrt(var + 1e-05)


def lanes_of(shape):
    return lax.broadcasted_iota(jnp.int32, shape, len(shape) - 1)


def doubled_projection(wdt_ref):
    d = wdt_ref[...]
    d = d - d[0:1, :]
    z = jnp.zeros_like(d)
    both = jnp.concatenate(
        [jnp.concatenate([d, z], axis=1), jnp.concatenate([z, d], axis=1)], axis=0
    )
    hi, lo = halves(both.T)
    return jnp.concatenate([hi, lo], axis=1)


def project(a, b, wp_ref):
    xh, xl = halves(jnp.concatenate([a, b], axis=1))
    p = mm(xh, wp_ref[...])
    return p[:, :128] + (p[:, 128:] + mm(xl, wp_ref[:, :128]))


def transition_kernel(
    pair_ref, tt_ref, wg_ref, wu_ref, wo_ref, wdt_ref, mid_ref, proj_ref, w1_ref, w2_ref, wp_ref
):
    step = pl.program_id(0)

    @pl.when(step == 0)
    def _():
        for k, ref in enumerate((wg_ref, wu_ref)):
            hi, lo = halves(ref[...])
            w1_ref[k, 0] = jnp.concatenate([hi, hi], axis=0)
            w1_ref[k, 1] = jnp.concatenate([lo, lo], axis=0)
        hi, lo = halves(wo_ref[...])
        w2_ref[...] = jnp.concatenate([hi, lo], axis=1)
        wp_ref[...] = doubled_projection(wdt_ref)

    x = pair_ref[...].reshape(1024, 128)
    nh, nl = halves(norm(x))
    both = jnp.concatenate([nh, nl], axis=1)
    out = jnp.zeros((1024, 128), F32)
    for c in range(0, 512, 256):
        gate = mm(both, w1_ref[0, 0, :, c : c + 256]) + mm(both, w1_ref[0, 1, :, c : c + 256])
        up = mm(both, w1_ref[1, 0, :, c : c + 256]) + mm(both, w1_ref[1, 1, :, c : c + 256])
        hidden = gate / (1.0 + jnp.exp(-gate)) * up
        hh, hl = halves(hidden)
        o = mm(hh, w2_ref[c : c + 256, :])
        out = out + (o[:, :128] + (o[:, 128:] + mm(hl, w2_ref[c : c + 256, :128])))
    mid = x + out
    mid_ref[...] = mid.reshape(4, 2, 4, 32, 128)
    split = mid.reshape(32, 2, 16, 128)
    proj = project(split[:, 0].reshape(512, 128), split[:, 1].reshape(512, 128), wp_ref)
    turned = pltpu.roll(tt_ref[...].astype(F32), (128 - 8 * step) % 128, 1)
    lane = lanes_of((16, 128))
    for k in range(4):
        for st in range(2):
            for w in range(4):
                i = k * 32 + st * 4 + w
                a = turned[0:16, i : i + 1]
                b = turned[16:32, i : i + 1]
                mark = jnp.where(lane == 0, a, jnp.where(lane == 64, b, 0.0))
                n = (k * 8 + st * 4 + w) * 16
                proj_ref[st, k, w] = proj[n : n + 16] + mark


def bias_kernel(mid_ref, wb_ref, bias_ref, w3_ref, n_ref):
    @pl.when(pl.program_id(0) == 0)
    def _():
        w = jnp.concatenate([wb_ref[...]] * 8, axis=1)
        lane = lanes_of((128, 128))
        for k in range(8):
            hi, lo = halves(jnp.where(lane // 16 == k, w, 0.0))
            row = jnp.concatenate([hi, lo], axis=1)
            w3_ref[k] = jnp.concatenate([row, row], axis=0)

    n_ref[...] = norm(mid_ref[...])
    acc = jnp.zeros((256, 256), F32)
    for k in range(8):
        x = jnp.concatenate(
            [n_ref[pl.ds(g * 8 + k, 64, stride=32), :] for g in range(4)], axis=0
        )
        hi, lo = halves(x)
        acc = acc + mm(jnp.concatenate([hi, lo], axis=1), w3_ref[k])
    acc = acc[:, :128] + acc[:, 128:]
    for g in range(4):
        bias_ref[:, g * 128 : (g + 1) * 128] = acc[g * 64 : (g + 1) * 64]


def pick_matrix():
    row = lax.broadcasted_iota(jnp.int32, (128, 128), 0)
    return jnp.where((row // 64 == lanes_of((128, 128)) // 64) & (row % 64 == 0), 1.0, 0.0).astype(BF16)


def own_kernel(proj_ref, bd_ref, own_ref, hits_ref):
    front = proj_ref[0:4, 0].reshape(256, 128)
    back = proj_ref[4:8, 0].reshape(256, 128)
    left = lanes_of((256, 128)) < 64
    own_a = jnp.where(left, front, pltpu.roll(back, 64, 1)).reshape(16, 16, 128)
    own_b = jnp.where(left, pltpu.roll(front, 64, 1), back).reshape(16, 16, 128)
    own = jnp.concatenate([own_a, own_b], axis=1).reshape(512, 128)
    bins = lanes_of((512, 128)) % 64
    mark = jnp.where(bins == 0, own, 0.0)
    target = mm(mark.astype(BF16), pick_matrix())
    bd = bd_ref[...]
    bd = bd - bd[:, 0:1]
    own_ref[...] = (own - mark + jnp.concatenate([bd, bd], axis=1)).reshape(16, 32, 128)
    hits = jnp.where(bins.astype(F32) == target, 1.0, 0.0).astype(BF16)
    hits_ref[...] = hits.reshape(16, 32, 128)


def attention_kernel(
    xr_ref, xc_ref, bias_ref, wq_ref, wk_ref, wv_ref, msg_ref, rowpad_ref, colpad_ref
):
    def tokens(ref, n):
        x = jnp.concatenate([ref[pl.ds(q, n, stride=4), :] for q in range(3)], axis=1)
        return norm(x), ref[pl.ds(3, n, stride=4), :][:, 0:1]

    rows, row_pad = tokens(xr_ref, 128)
    cols, col_pad = tokens(xc_ref, 32)
    lane = lanes_of((16, 128))
    for m in range(4):
        a = row_pad[m * 32 : m * 32 + 16]
        b = row_pad[m * 32 + 16 : m * 32 + 32]
        rowpad_ref[m * 16 : (m + 1) * 16, :] = jnp.where(lane < 64, a, b)
    colpad_ref[...] = jnp.broadcast_to(col_pad, (32, 128))
    query = mm3(rows, wq_ref[...]) * (24.0**-0.5)
    key = mm3(cols, wk_ref[...])
    value = mm3(cols, wv_ref[...])
    of_head = lanes_of((16, 384)) // 24 == lax.broadcasted_iota(jnp.int32, (16, 384), 0)

    def spread(y):
        return jnp.where(of_head[None], y[:, None, :], 0.0).reshape(512, 384)

    scores = mm3(query, spread(key), mm_nt) + bias_ref[...]
    of_key = lanes_of((32, 512)) // 16 == lax.broadcasted_iota(jnp.int32, (32, 512), 0)
    pad_lane = jnp.sum(jnp.where(of_key, col_pad, 0.0), axis=0, keepdims=True)
    scores = jnp.where(pad_lane > 0.5, scores, -1000000000.0)

    def over_keys(y, op):
        r = op(op(y[:, :128], y[:, 128:256]), op(y[:, 256:384], y[:, 384:]))
        for shift in (16, 32, 64):
            r = op(r, pltpu.roll(r, shift, 1))
        return r

    top = over_keys(scores, jnp.maximum)
    expo = jnp.exp(scores - jnp.concatenate([top] * 4, axis=1))
    total = over_keys(expo, jnp.add)
    acc = mm3(expo, spread(value))
    lane = lanes_of((128, 128))
    tail = jnp.where(lane < 16, total, jnp.where(lane < 32, top, 0.0))
    for q in range(3):
        msg_ref[pl.ds(q, 128, stride=4), :] = acc[:, q * 128 : (q + 1) * 128]
    msg_ref[pl.ds(3, 128, stride=4), :] = tail


def merge_kernel(msg_ref, single_ref, wg_ref, wo_ref, out_ref):
    lane = lanes_of((32, 128))
    accs, factors, totals = [], [], []
    for t in range(4):
        part = [msg_ref[pl.ds(4 * t + q, 32, stride=16), :] for q in range(4)]
        accs.append(jnp.concatenate(part[:3], axis=1))
        tail = part[3]
        local = pltpu.roll(tail, 112, 1)
        top = jnp.max(local, axis=0, keepdims=True)
        f = jnp.where(lane < 16, jnp.exp(local - top), 0.0)
        factors.append(f)
        totals.append(jnp.sum(f * tail, axis=0, keepdims=True))
    expand = jnp.where(
        lanes_of((128, 384)) // 24 == lax.broadcasted_iota(jnp.int32, (128, 384), 0), 1.0, 0.0
    )
    stacked = jnp.concatenate(factors + totals + totals, axis=0)
    wide = jnp.dot(stacked, expand, precision=lax.Precision.HIGHEST, preferred_element_type=F32)
    rows = []
    for t in range(4):
        num = jnp.sum(wide[t * 32 : (t + 1) * 32] * accs[t], axis=0, keepdims=True)
        rows.append(num / wide[128 + t : 129 + t])
    attended = jnp.concatenate(rows, axis=0)
    single = single_ref[...]
    g = mm3(norm(single), wg_ref[...])
    out_ref[...] = single + mm3(attended / (1.0 + jnp.exp(-g)), wo_ref[...])


def gradient_kernel(place_ref, *refs):
    parts = refs[:8]
    own_ref, hits_ref, mid_ref, rowpad_ref, colpad_ref, wdt_ref, out_ref = refs[8:15]
    f_ref, w_ref, ones_ref, pick_ref, d_ref = refs[15:]

    @pl.when(pl.program_id(0) == 0)
    def _():
        d = wdt_ref[...]
        z = jnp.zeros_like(d)
        both = jnp.concatenate(
            [jnp.concatenate([d, z], axis=1), jnp.concatenate([z, d], axis=1)], axis=0
        )
        hi, lo = halves(both)
        w_ref[0] = jnp.concatenate([hi, hi], axis=0)
        w_ref[1] = jnp.concatenate([lo, lo], axis=0)
        row = lax.broadcasted_iota(jnp.int32, (256, 128), 0) % 128
        same = row // 64 == lanes_of((256, 128)) // 64
        ones_ref[...] = jnp.where(same, 1.0, 0.0).astype(BF16)
        pick_ref[...] = pick_matrix()

    for p in range(8):
        place = place_ref[0] ^ p
        f_ref[pl.ds(pl.multiple_of(place * 64, 64), 64), :] = parts[p][0]

    lane = lanes_of((512, 128))
    first = lane < 64
    bins = lane % 64
    flip = jnp.concatenate([f_ref[pl.ds(i, 32, stride=16), :] for i in range(16)], axis=0)
    mark = jnp.where(bins == 0, flip, 0.0)
    target = mm(mark.astype(BF16), pick_ref[...])
    logits = own_ref[...].reshape(512, 128) + (flip - mark)
    top_a = jnp.max(jnp.where(first, logits, -3.0e38), axis=-1, keepdims=True)
    top_b = jnp.max(jnp.where(first, -3.0e38, logits), axis=-1, keepdims=True)
    expo = jnp.exp(logits - jnp.where(first, top_a, top_b))
    hi, lo = halves(expo)
    total = mm(jnp.concatenate([hi, lo], axis=1), ones_ref[...])
    hits = jnp.where(bins.astype(F32) == target, 1.0, 0.0) + hits_ref[...].reshape(512, 128).astype(F32)
    mask = rowpad_ref[...][:, None, :] * colpad_ref[...][None]
    hi, lo = halves(mask.reshape(512, 128) * (expo * (2.0 / total) - hits))
    d_ref[...] = jnp.concatenate([hi, lo], axis=1)
    change = mm(d_ref[...], w_ref[0]) + mm(d_ref[...], w_ref[1])
    for k in range(2):
        out_ref[0, k] = mid_ref[0, k] + change[:, k * 128 : (k + 1) * 128].reshape(16, 32, 128)


def tokens_kernel(single_ref, pad_ref, out_ref):
    tile = []
    for t in range(4):
        for q in range(3):
            tile.append(single_ref[t : t + 1, q * 128 : (q + 1) * 128])
        tile.append(jnp.full((1, 128), pad_ref[t].astype(F32)))
    out_ref[...] = jnp.broadcast_to(jnp.concatenate(tile, axis=0)[None], (32, 16, 128))


def full(shape):
    return pl.BlockSpec(shape, lambda *_: (0,) * len(shape))


def struct(*shape):
    return jax.ShapeDtypeStruct(shape, F32)


def per_device(
    pair,
    single,
    target_bins,
    token_pad,
    w_gate,
    w_up,
    w_out,
    w_bias,
    w_query,
    w_key,
    w_value,
    w_gating,
    w_attn_out,
    w_dist,
    b_dist,
):
    at = {name: lax.axis_index(name) for name in ALL}
    coords = all_coords()
    tt = target_bins.T
    wdt = w_dist.T

    tok = pl.pallas_call(
        tokens_kernel,
        in_specs=[full((4, 384)), pl.BlockSpec(memory_space=pltpu.SMEM)],
        out_shape=struct(32, 16, 128),
        name="tokens",
    )(single, token_pad)
    rows_tok = lax.all_to_all(tok, COL, split_axis=0, concat_axis=0, tiled=True)
    rows_tok = rows_tok.reshape(512, 128)

    mid, proj = pl.pallas_call(
        transition_kernel,
        grid=(4,),
        in_specs=[
            pl.BlockSpec((4, 2, 4, 32, 128), lambda s: (0, s, 0, 0, 0)),
            full((32, 128)),
            full((128, 512)),
            full((128, 512)),
            full((512, 128)),
            full((64, 128)),
        ],
        out_specs=[
            pl.BlockSpec((4, 2, 4, 32, 128), lambda s: (0, s, 0, 0, 0)),
            pl.BlockSpec((2, 4, 4, 16, 128), lambda s: (s, 0, 0, 0, 0)),
        ],
        out_shape=[struct(4, 8, 4, 32, 128), struct(8, 4, 4, 16, 128)],
        scratch_shapes=[
            pltpu.VMEM((2, 2, 256, 512), BF16),
            pltpu.VMEM((512, 256), BF16),
            pltpu.VMEM((256, 256), BF16),
        ],
        name="transition",
    )(pair.reshape(4, 8, 4, 32, 128), tt, w_gate, w_up, w_out, wdt)

    spread = lax.all_to_all(
        proj.reshape(32, 64, 128), PLANE, split_axis=0, concat_axis=0, tiled=True
    ).reshape(8, 4, 64, 128)

    quarter = lax.dynamic_slice_in_dim(rows_tok, (at["yl"] * 2 + at["core"]) * 128, 128, 0)
    perm = [(flat_index(c), flat_index((c[2], c[3], c[0], c[1], c[4], c[5]))) for c in coords]
    cols_tok = lax.ppermute(quarter, ALL, perm)

    bias = pl.pallas_call(
        bias_kernel,
        grid=(2,),
        in_specs=[pl.BlockSpec((2048, 128), lambda m: (m, 0)), full((128, 16))],
        out_specs=pl.BlockSpec((64, 512), lambda m: (m, 0)),
        out_shape=struct(128, 512),
        scratch_shapes=[pltpu.VMEM((8, 256, 256), BF16), pltpu.VMEM((2048, 128), F32)],
        name="bias",
    )(mid.reshape(4096, 128), w_bias)

    own, hits = pl.pallas_call(
        own_kernel,
        grid=(4,),
        in_specs=[pl.BlockSpec((8, 1, 4, 16, 128), lambda m: (0, m, 0, 0, 0)), full((1, 64))],
        out_specs=[pl.BlockSpec((16, 32, 128), lambda m: (m, 0, 0))] * 2,
        out_shape=[struct(64, 32, 128), jax.ShapeDtypeStruct((64, 32, 128), BF16)],
        name="own",
    )(proj, b_dist[None])

    msg, rowpad, colpad = pl.pallas_call(
        attention_kernel,
        out_shape=[struct(512, 128), struct(64, 128), struct(32, 128)],
        name="attention",
    )(rows_tok, cols_tok, bias, w_query, w_key, w_value)

    parts = []
    for n in range(8):
        u, v = n // 2, n % 2
        piece = lax.dynamic_index_in_dim(
            spread, (at["x"] ^ u) * 2 + (at["yh"] ^ v), 0, keepdims=False
        )
        perm = []
        for c in coords:
            x, zh, zl, yh, yl, core = c
            perm.append((flat_index(c), flat_index((zl, yh ^ v, x ^ u, zh, yl, core))))
        parts.append(lax.ppermute(piece, ALL, perm))
    place = (at["zl"] * 2 + at["zh"]).reshape(1)

    merged = lax.all_to_all(msg.reshape(32, 16, 128), COL, split_axis=0, concat_axis=0, tiled=True)
    merged = merged.reshape(512, 128)
    single_out = pl.pallas_call(
        merge_kernel, out_shape=struct(4, 384), name="merge"
    )(merged, single, w_gating, w_attn_out)

    grouped = pl.BlockSpec((1, 2, 16, 32, 128), lambda m, _: (m, 0, 0, 0, 0))
    pair_out = pl.pallas_call(
        gradient_kernel,
        grid_spec=pltpu.PrefetchScalarGridSpec(
            num_scalar_prefetch=1,
            grid=(4,),
            in_specs=[pl.BlockSpec((1, 64, 128), lambda m, _: (m, 0, 0))] * 8
            + [
                pl.BlockSpec((16, 32, 128), lambda m, _: (m, 0, 0)),
                pl.BlockSpec((16, 32, 128), lambda m, _: (m, 0, 0)),
                grouped,
                pl.BlockSpec((16, 128), lambda m, _: (m, 0)),
                full((32, 128)),
                full((64, 128)),
            ],
            out_specs=grouped,
            scratch_shapes=[
                pltpu.VMEM((512, 128), F32),
                pltpu.VMEM((2, 256, 256), BF16),
                pltpu.VMEM((256, 128), BF16),
                pltpu.VMEM((128, 128), BF16),
                pltpu.VMEM((512, 256), BF16),
            ],
        ),
        out_shape=struct(4, 2, 16, 32, 128),
        name="gradient",
    )(
        place,
        *parts,
        own,
        hits,
        mid.reshape(4, 2, 16, 32, 128),
        rowpad,
        colpad,
        wdt,
    )
    pair_out = pair_out.reshape(128, 32, 128)
    return (pair_out, single_out)


def solution(mesh):
    fine = Mesh(mesh.devices.reshape(SIZES), ALL)
    row, col = ("x", "zh"), COL
    in_specs = (
        P(row, col, None),
        P(ALL, None),
        P(row, col),
        P(ALL),
    ) + (P(),) * 11
    out_specs = (P(row, col, None), P(ALL, None))
    return jax.shard_map(
        per_device, mesh=fine, in_specs=in_specs, out_specs=out_specs, check_vma=False
    )
```

```python
import jax
import jax.numpy as jnp
from jax import lax
from jax.experimental import pallas as pl
from jax.experimental.pallas import tpu as pltpu
from jax.sharding import Mesh, PartitionSpec as P


F32 = jnp.float32
BF16 = jnp.bfloat16
ALL = ("x", "zh", "zl", "yh", "yl", "core")
COL = ("zl", "yh", "yl", "core")
PLANE = ("x", "yh", "yl", "core")
SIZES = (4, 2, 4, 2, 2, 2)


def flat_index(coords):
    index = 0
    for c, n in zip(coords, SIZES):
        index = index * n + c
    return index


def all_coords():
    out = [()]
    for n in SIZES:
        out = [c + (k,) for c in out for k in range(n)]
    return out


def halves(x):
    hi = x.astype(BF16)
    lo = (x - hi.astype(F32)).astype(BF16)
    return hi, lo


def mm(a, b):
    return jnp.dot(a, b, preferred_element_type=F32)


def mm_nt(a, b):
    return lax.dot_general(a, b, (((1,), (1,)), ((), ())), preferred_element_type=F32)


def mm3(a, b, dot=mm):
    ah, al = halves(a)
    bh, bl = halves(b)
    return dot(ah, bh) + (dot(al, bh) + dot(ah, bl))


def norm(x):
    mean = jnp.mean(x, axis=-1, keepdims=True)
    centred = x - mean
    var = jnp.mean(centred * centred, axis=-1, keepdims=True)
    return centred * lax.rsqrt(var + 1e-05)


def lanes_of(shape):
    return lax.broadcasted_iota(jnp.int32, shape, len(shape) - 1)


def doubled_projection(wdt_ref):
    d = wdt_ref[...]
    d = d - d[0:1, :]
    z = jnp.zeros_like(d)
    both = jnp.concatenate(
        [jnp.concatenate([d, z], axis=1), jnp.concatenate([z, d], axis=1)], axis=0
    )
    hi, lo = halves(both.T)
    return jnp.concatenate([hi, lo], axis=1)


def project(a, b, wp_ref):
    xh, xl = halves(jnp.concatenate([a, b], axis=1))
    p = mm(xh, wp_ref[...])
    return p[:, :128] + (p[:, 128:] + mm(xl, wp_ref[:, :128]))


def transition_kernel(
    pair_ref,
    tt_ref,
    wg_ref,
    wu_ref,
    wo_ref,
    wdt_ref,
    bd_ref,
    mid_ref,
    proj_ref,
    own_ref,
    hits_ref,
    w1_ref,
    w2_ref,
    wp_ref,
):
    step = pl.program_id(0)

    @pl.when(step == 0)
    def _():
        for k, ref in enumerate((wg_ref, wu_ref)):
            hi, lo = halves(ref[...])
            w1_ref[k, 0] = jnp.concatenate([hi, hi], axis=0)
            w1_ref[k, 1] = jnp.concatenate([lo, lo], axis=0)
        hi, lo = halves(wo_ref[...])
        w2_ref[...] = jnp.concatenate([hi, lo], axis=1)
        wp_ref[...] = doubled_projection(wdt_ref)

    x = pair_ref[...].reshape(1024, 128)
    nh, nl = halves(norm(x))
    both = jnp.concatenate([nh, nl], axis=1)
    out = jnp.zeros((1024, 128), F32)
    for c in range(0, 512, 256):
        gate = mm(both, w1_ref[0, 0, :, c : c + 256]) + mm(both, w1_ref[0, 1, :, c : c + 256])
        up = mm(both, w1_ref[1, 0, :, c : c + 256]) + mm(both, w1_ref[1, 1, :, c : c + 256])
        hidden = gate / (1.0 + jnp.exp(-gate)) * up
        hh, hl = halves(hidden)
        o = mm(hh, w2_ref[c : c + 256, :])
        out = out + (o[:, :128] + (o[:, 128:] + mm(hl, w2_ref[c : c + 256, :128])))
    mid = x + out
    mid_ref[...] = mid.reshape(4, 2, 1, 4, 32, 128)
    split = mid.reshape(32, 2, 16, 128)
    proj = project(split[:, 0].reshape(512, 128), split[:, 1].reshape(512, 128), wp_ref)
    turned = pltpu.roll(tt_ref[...].astype(F32), (128 - 4 * step) % 128, 1)
    lane = lanes_of((16, 128))
    left = lane < 64
    at_zero = lane % 64 == 0
    number = (lane % 64).astype(F32)
    bd = bd_ref[...]
    bd = bd - bd[:, 0:1]
    bd = jnp.concatenate([bd, bd], axis=1)
    for k in range(4):
        for w in range(4):
            tile, front, back = [], [], []
            for ih in range(2):
                i = k * 32 + ih * 16 + w
                a = jnp.broadcast_to(turned[0:16, i : i + 1], (16, 128))
                b = jnp.broadcast_to(turned[16:32, i : i + 1], (16, 128))
                n = (k * 8 + ih * 4 + w) * 16
                p = proj[n : n + 16]
                proj_ref[ih, 0, k, w] = jnp.where(at_zero, jnp.where(left, a, b), p)
                tile.append(p)
                front.append(a)
                back.append(b)
            own_ref[k, 0, w, 0:16] = jnp.where(left, tile[0], pltpu.roll(tile[1], 64, 1)) + bd
            own_ref[k, 0, w, 16:32] = jnp.where(left, pltpu.roll(tile[0], 64, 1), tile[1]) + bd
            hit = [
                jnp.where(number == jnp.where(left, t[0], t[1]), 1.0, 0.0) for t in (front, back)
            ]
            hits_ref[k, 0, w] = jnp.concatenate(hit, axis=0).astype(BF16)


def bias_kernel(mid_ref, wb_ref, bias_ref, w3_ref, n_ref):
    @pl.when(pl.program_id(0) == 0)
    def _():
        w = jnp.concatenate([wb_ref[...]] * 8, axis=1)
        lane = lanes_of((128, 128))
        for k in range(8):
            hi, lo = halves(jnp.where(lane // 16 == k, w, 0.0))
            row = jnp.concatenate([hi, lo], axis=1)
            w3_ref[k] = jnp.concatenate([row, row], axis=0)

    n_ref[...] = norm(mid_ref[...])
    acc = jnp.zeros((256, 256), F32)
    for k in range(8):
        x = jnp.concatenate(
            [n_ref[pl.ds(g * 8 + k, 64, stride=32), :] for g in range(4)], axis=0
        )
        hi, lo = halves(x)
        acc = acc + mm(jnp.concatenate([hi, lo], axis=1), w3_ref[k])
    acc = acc[:, :128] + acc[:, 128:]
    for g in range(4):
        bias_ref[:, g * 128 : (g + 1) * 128] = acc[g * 64 : (g + 1) * 64]


def pick_matrix():
    row = lax.broadcasted_iota(jnp.int32, (128, 128), 0)
    return jnp.where((row // 64 == lanes_of((128, 128)) // 64) & (row % 64 == 0), 1.0, 0.0).astype(BF16)


def attention_kernel(
    xr_ref,
    xc_ref,
    bias_ref,
    wq_ref,
    wk_ref,
    wv_ref,
    single_ref,
    wg_ref,
    msg_ref,
    rowpad_ref,
    colpad_ref,
    gate_ref,
):
    gate_ref[...] = 1.0 / (1.0 + jnp.exp(-mm3(norm(single_ref[...]), wg_ref[...])))

    def tokens(ref, n):
        x = jnp.concatenate([ref[pl.ds(q, n, stride=4), :] for q in range(3)], axis=1)
        return norm(x), ref[pl.ds(3, n, stride=4), :][:, 0:1]

    rows, row_pad = tokens(xr_ref, 128)
    cols, col_pad = tokens(xc_ref, 32)
    lane = lanes_of((16, 128))
    for m in range(4):
        a = row_pad[m * 32 : m * 32 + 16]
        b = row_pad[m * 32 + 16 : m * 32 + 32]
        rowpad_ref[m * 16 : (m + 1) * 16, :] = jnp.where(lane < 64, a, b)
    colpad_ref[...] = jnp.broadcast_to(col_pad, (32, 128))
    query = mm3(rows, wq_ref[...]) * (24.0**-0.5)
    key = mm3(cols, wk_ref[...])
    value = mm3(cols, wv_ref[...])
    of_head = lanes_of((16, 384)) // 24 == lax.broadcasted_iota(jnp.int32, (16, 384), 0)

    def spread(y):
        return jnp.where(of_head[None], y[:, None, :], 0.0).reshape(512, 384)

    scores = mm3(query, spread(key), mm_nt) + bias_ref[...]
    of_key = lanes_of((32, 512)) // 16 == lax.broadcasted_iota(jnp.int32, (32, 512), 0)
    pad_lane = jnp.sum(jnp.where(of_key, col_pad, 0.0), axis=0, keepdims=True)
    scores = jnp.where(pad_lane > 0.5, scores, -1000000000.0)

    def over_keys(y, op):
        r = op(op(y[:, :128], y[:, 128:256]), op(y[:, 256:384], y[:, 384:]))
        for shift in (16, 32, 64):
            r = op(r, pltpu.roll(r, shift, 1))
        return r

    top = over_keys(scores, jnp.maximum)
    expo = jnp.exp(scores - jnp.concatenate([top] * 4, axis=1))
    total = over_keys(expo, jnp.add)
    acc = mm3(expo, spread(value))
    lane = lanes_of((128, 128))
    tail = jnp.where(lane < 16, total, jnp.where(lane < 32, top, 0.0))
    for q in range(3):
        msg_ref[pl.ds(q, 128, stride=4), :] = acc[:, q * 128 : (q + 1) * 128]
    msg_ref[pl.ds(3, 128, stride=4), :] = tail


def merge_tokens(msg_ref, single_ref, gate_ref, wo_ref, out_ref):
    lane = lanes_of((32, 128))
    accs, factors, totals = [], [], []
    for t in range(4):
        part = [msg_ref[pl.ds(4 * t + q, 32, stride=16), :] for q in range(4)]
        accs.append(jnp.concatenate(part[:3], axis=1))
        tail = part[3]
        local = pltpu.roll(tail, 112, 1)
        top = jnp.max(local, axis=0, keepdims=True)
        f = jnp.where(lane < 16, jnp.exp(local - top), 0.0)
        factors.append(f)
        totals.append(jnp.sum(f * tail, axis=0, keepdims=True))
    expand = jnp.where(
        lanes_of((128, 384)) // 24 == lax.broadcasted_iota(jnp.int32, (128, 384), 0), 1.0, 0.0
    )
    stacked = jnp.concatenate(factors + totals + totals, axis=0)
    wide = jnp.dot(stacked, expand, precision=lax.Precision.HIGHEST, preferred_element_type=F32)
    rows = []
    for t in range(4):
        num = jnp.sum(wide[t * 32 : (t + 1) * 32] * accs[t], axis=0, keepdims=True)
        rows.append(num / wide[128 + t : 129 + t])
    attended = jnp.concatenate(rows, axis=0)
    out_ref[...] = single_ref[...] + mm3(gate_ref[...] * attended, wo_ref[...])


def gradient_kernel(place_ref, *refs):
    parts = refs[:8]
    own_ref, hits_ref, mid_ref, rowpad_ref, colpad_ref, wdt_ref = refs[8:14]
    msg_ref, single_ref, gate_ref, wo_ref, out_ref, single_out_ref = refs[14:20]
    f_ref, w_ref, ones_ref, pick_ref, d_ref = refs[20:]

    @pl.when(pl.program_id(0) == 0)
    def _():
        d = wdt_ref[...]
        z = jnp.zeros_like(d)
        both = jnp.concatenate(
            [jnp.concatenate([d, z], axis=1), jnp.concatenate([z, d], axis=1)], axis=0
        )
        hi, lo = halves(both)
        w_ref[0] = jnp.concatenate([hi, hi], axis=0)
        w_ref[1] = jnp.concatenate([lo, lo], axis=0)
        row = lax.broadcasted_iota(jnp.int32, (256, 128), 0) % 128
        same = row // 64 == lanes_of((256, 128)) // 64
        ones_ref[...] = jnp.where(same, 1.0, 0.0).astype(BF16)
        pick_ref[...] = pick_matrix()

    for p in range(8):
        place = place_ref[0] ^ p
        f_ref[pl.ds(pl.multiple_of(place * 64, 64), 64), :] = parts[p][0]

    lane = lanes_of((512, 128))
    first = lane < 64
    bins = lane % 64
    flip = jnp.concatenate([f_ref[pl.ds(i, 32, stride=16), :] for i in range(16)], axis=0)
    mark = jnp.where(bins == 0, flip, 0.0)
    target = mm(mark.astype(BF16), pick_ref[...])
    logits = own_ref[...].reshape(512, 128) + (flip - mark)
    top_a = jnp.max(jnp.where(first, logits, -3.0e38), axis=-1, keepdims=True)
    top_b = jnp.max(jnp.where(first, -3.0e38, logits), axis=-1, keepdims=True)
    expo = jnp.exp(logits - jnp.where(first, top_a, top_b))
    hi, lo = halves(expo)
    total = mm(jnp.concatenate([hi, lo], axis=1), ones_ref[...])
    hits = jnp.where(bins.astype(F32) == target, 1.0, 0.0) + hits_ref[...].reshape(512, 128).astype(F32)
    mask = rowpad_ref[...][:, None, :] * colpad_ref[...][None]
    hi, lo = halves(mask.reshape(512, 128) * (expo * (2.0 / total) - hits))
    d_ref[...] = jnp.concatenate([hi, lo], axis=1)
    change = mm(d_ref[...], w_ref[0]) + mm(d_ref[...], w_ref[1])
    for k in range(2):
        out_ref[0, k] = mid_ref[0, k] + change[:, k * 128 : (k + 1) * 128].reshape(16, 32, 128)

    @pl.when(pl.program_id(0) == 3)
    def _():
        merge_tokens(msg_ref, single_ref, gate_ref, wo_ref, single_out_ref)


def tokens_kernel(single_ref, pad_ref, out_ref):
    tile = []
    for t in range(4):
        for q in range(3):
            tile.append(single_ref[t : t + 1, q * 128 : (q + 1) * 128])
        tile.append(jnp.full((1, 128), pad_ref[t].astype(F32)))
    out_ref[...] = jnp.broadcast_to(jnp.concatenate(tile, axis=0)[None], (32, 16, 128))


def full(shape):
    return pl.BlockSpec(shape, lambda *_: (0,) * len(shape))


def struct(*shape):
    return jax.ShapeDtypeStruct(shape, F32)


def per_device(
    pair,
    single,
    target_bins,
    token_pad,
    w_gate,
    w_up,
    w_out,
    w_bias,
    w_query,
    w_key,
    w_value,
    w_gating,
    w_attn_out,
    w_dist,
    b_dist,
):
    at = {name: lax.axis_index(name) for name in ALL}
    coords = all_coords()
    tt = target_bins.T
    wdt = w_dist.T

    tok = pl.pallas_call(
        tokens_kernel,
        in_specs=[full((4, 384)), pl.BlockSpec(memory_space=pltpu.SMEM)],
        out_shape=struct(32, 16, 128),
        name="tokens",
    )(single, token_pad)
    rows_tok = lax.all_to_all(tok, COL, split_axis=0, concat_axis=0, tiled=True)
    rows_tok = rows_tok.reshape(512, 128)

    mid, proj, own, hits = pl.pallas_call(
        transition_kernel,
        grid=(4,),
        in_specs=[
            pl.BlockSpec((4, 2, 1, 4, 32, 128), lambda s: (0, 0, s, 0, 0, 0)),
            full((32, 128)),
            full((128, 512)),
            full((128, 512)),
            full((512, 128)),
            full((64, 128)),
            full((1, 64)),
        ],
        out_specs=[
            pl.BlockSpec((4, 2, 1, 4, 32, 128), lambda s: (0, 0, s, 0, 0, 0)),
            pl.BlockSpec((2, 1, 4, 4, 16, 128), lambda s: (0, s, 0, 0, 0, 0)),
            pl.BlockSpec((4, 1, 4, 32, 128), lambda s: (0, s, 0, 0, 0)),
            pl.BlockSpec((4, 1, 4, 32, 128), lambda s: (0, s, 0, 0, 0)),
        ],
        out_shape=[
            struct(4, 2, 4, 4, 32, 128),
            struct(2, 4, 4, 4, 16, 128),
            struct(4, 4, 4, 32, 128),
            jax.ShapeDtypeStruct((4, 4, 4, 32, 128), BF16),
        ],
        scratch_shapes=[
            pltpu.VMEM((2, 2, 256, 512), BF16),
            pltpu.VMEM((512, 256), BF16),
            pltpu.VMEM((256, 256), BF16),
        ],
        name="transition",
    )(pair.reshape(4, 2, 4, 4, 32, 128), tt, w_gate, w_up, w_out, wdt, b_dist[None])

    spread = lax.all_to_all(
        proj.reshape(32, 64, 128), PLANE, split_axis=0, concat_axis=0, tiled=True
    ).reshape(8, 4, 64, 128)

    quarter = lax.dynamic_slice_in_dim(rows_tok, (at["yl"] * 2 + at["core"]) * 128, 128, 0)
    perm = [(flat_index(c), flat_index((c[2], c[3], c[0], c[1], c[4], c[5]))) for c in coords]
    cols_tok = lax.ppermute(quarter, ALL, perm)

    bias = pl.pallas_call(
        bias_kernel,
        grid=(2,),
        in_specs=[pl.BlockSpec((2048, 128), lambda m: (m, 0)), full((128, 16))],
        out_specs=pl.BlockSpec((64, 512), lambda m: (m, 0)),
        out_shape=struct(128, 512),
        scratch_shapes=[pltpu.VMEM((8, 256, 256), BF16), pltpu.VMEM((2048, 128), F32)],
        name="bias",
    )(mid.reshape(4096, 128), w_bias)

    msg, rowpad, colpad, gate = pl.pallas_call(
        attention_kernel,
        out_shape=[struct(512, 128), struct(64, 128), struct(32, 128), struct(4, 384)],
        name="attention",
    )(rows_tok, cols_tok, bias, w_query, w_key, w_value, single, w_gating)

    parts = []
    for n in range(8):
        u, v = n // 2, n % 2
        piece = lax.dynamic_index_in_dim(
            spread, (at["x"] ^ u) * 2 + (at["yh"] ^ v), 0, keepdims=False
        )
        perm = []
        for c in coords:
            x, zh, zl, yh, yl, core = c
            perm.append((flat_index(c), flat_index((zl, yh ^ v, x ^ u, zh, yl, core))))
        parts.append(lax.ppermute(piece, ALL, perm))
    place = (at["zl"] * 2 + at["zh"]).reshape(1)

    merged = lax.all_to_all(msg.reshape(32, 16, 128), COL, split_axis=0, concat_axis=0, tiled=True)
    merged = merged.reshape(512, 128)
    grouped = pl.BlockSpec((1, 2, 16, 32, 128), lambda m, _: (m, 0, 0, 0, 0))
    pair_out, single_out = pl.pallas_call(
        gradient_kernel,
        grid_spec=pltpu.PrefetchScalarGridSpec(
            num_scalar_prefetch=1,
            grid=(4,),
            in_specs=[pl.BlockSpec((1, 64, 128), lambda m, _: (m, 0, 0))] * 8
            + [
                pl.BlockSpec((16, 32, 128), lambda m, _: (m, 0, 0)),
                pl.BlockSpec((16, 32, 128), lambda m, _: (m, 0, 0)),
                grouped,
                pl.BlockSpec((16, 128), lambda m, _: (m, 0)),
                full((32, 128)),
                full((64, 128)),
                full((512, 128)),
                full((4, 384)),
                full((4, 384)),
                full((384, 384)),
            ],
            out_specs=[grouped, full((4, 384))],
            scratch_shapes=[
                pltpu.VMEM((512, 128), F32),
                pltpu.VMEM((2, 256, 256), BF16),
                pltpu.VMEM((256, 128), BF16),
                pltpu.VMEM((128, 128), BF16),
                pltpu.VMEM((512, 256), BF16),
            ],
        ),
        out_shape=[struct(4, 2, 16, 32, 128), struct(4, 384)],
        name="gradient",
    )(
        place,
        *parts,
        own.reshape(64, 32, 128),
        hits.reshape(64, 32, 128),
        mid.reshape(4, 2, 16, 32, 128),
        rowpad,
        colpad,
        wdt,
        merged,
        single,
        gate,
        w_attn_out,
    )
    pair_out = pair_out.reshape(128, 32, 128)
    return (pair_out, single_out)


def solution(mesh):
    fine = Mesh(mesh.devices.reshape(SIZES), ALL)
    row, col = ("x", "zh"), COL
    in_specs = (
        P(row, col, None),
        P(ALL, None),
        P(row, col),
        P(ALL),
    ) + (P(),) * 11
    out_specs = (P(row, col, None), P(ALL, None))
    return jax.shard_map(
        per_device, mesh=fine, in_specs=in_specs, out_specs=out_specs, check_vma=False
    )
```

```python
import jax
import jax.numpy as jnp
from jax import lax
from jax.experimental import pallas as pl
from jax.experimental.pallas import tpu as pltpu
from jax.sharding import Mesh, PartitionSpec as P


F32 = jnp.float32
BF16 = jnp.bfloat16
ALL = ("x", "zh", "zl", "yh", "yl", "core")
COL = ("zl", "yh", "yl", "core")
PLANE = ("x", "yh", "yl", "core")
SIZES = (4, 2, 4, 2, 2, 2)


def flat_index(coords):
    index = 0
    for c, n in zip(coords, SIZES):
        index = index * n + c
    return index


def all_coords():
    out = [()]
    for n in SIZES:
        out = [c + (k,) for c in out for k in range(n)]
    return out


def halves(x):
    hi = x.astype(BF16)
    lo = (x - hi.astype(F32)).astype(BF16)
    return hi, lo


def mm(a, b):
    return jnp.dot(a, b, preferred_element_type=F32)


def mm_nt(a, b):
    return lax.dot_general(a, b, (((1,), (1,)), ((), ())), preferred_element_type=F32)


def mm3(a, b, dot=mm):
    ah, al = halves(a)
    bh, bl = halves(b)
    return dot(ah, bh) + (dot(al, bh) + dot(ah, bl))


def norm(x):
    mean = jnp.mean(x, axis=-1, keepdims=True)
    centred = x - mean
    var = jnp.mean(centred * centred, axis=-1, keepdims=True)
    return centred * lax.rsqrt(var + 1e-05)


def lanes_of(shape):
    return lax.broadcasted_iota(jnp.int32, shape, len(shape) - 1)


def doubled_projection(wdt_ref):
    d = wdt_ref[...]
    d = d - d[0:1, :]
    z = jnp.zeros_like(d)
    both = jnp.concatenate(
        [jnp.concatenate([d, z], axis=1), jnp.concatenate([z, d], axis=1)], axis=0
    )
    hi, lo = halves(both.T)
    return jnp.concatenate([hi, lo], axis=1)


def project(a, b, wp_ref):
    xh, xl = halves(jnp.concatenate([a, b], axis=1))
    p = mm(xh, wp_ref[...])
    return p[:, :128] + (p[:, 128:] + mm(xl, wp_ref[:, :128]))


def transition_kernel(
    pair_ref,
    tt_ref,
    wg_ref,
    wu_ref,
    wo_ref,
    wdt_ref,
    bd_ref,
    mid_ref,
    proj_ref,
    own_ref,
    hits_ref,
    w1_ref,
    w2_ref,
    wp_ref,
):
    step = pl.program_id(0)

    @pl.when(step == 0)
    def _():
        for k, ref in enumerate((wg_ref, wu_ref)):
            hi, lo = halves(ref[...])
            w1_ref[k, 0] = jnp.concatenate([hi, hi], axis=0)
            w1_ref[k, 1] = jnp.concatenate([lo, lo], axis=0)
        hi, lo = halves(wo_ref[...])
        w2_ref[...] = jnp.concatenate([hi, lo], axis=1)
        wp_ref[...] = doubled_projection(wdt_ref)

    x = pair_ref[...].reshape(1024, 128)
    nh, nl = halves(norm(x))
    both = jnp.concatenate([nh, nl], axis=1)
    out = jnp.zeros((1024, 128), F32)
    for c in range(0, 512, 256):
        gate = mm(both, w1_ref[0, 0, :, c : c + 256]) + mm(both, w1_ref[0, 1, :, c : c + 256])
        up = mm(both, w1_ref[1, 0, :, c : c + 256]) + mm(both, w1_ref[1, 1, :, c : c + 256])
        hidden = gate / (1.0 + jnp.exp(-gate)) * up
        hh, hl = halves(hidden)
        o = mm(hh, w2_ref[c : c + 256, :])
        out = out + (o[:, :128] + (o[:, 128:] + mm(hl, w2_ref[c : c + 256, :128])))
    mid = x + out
    mid_ref[...] = mid.reshape(4, 2, 1, 4, 32, 128)
    split = mid.reshape(32, 2, 16, 128)
    proj = project(split[:, 0].reshape(512, 128), split[:, 1].reshape(512, 128), wp_ref)
    turned = pltpu.roll(tt_ref[...].astype(F32), (128 - 4 * step) % 128, 1)
    lane = lanes_of((16, 128))
    left = lane < 64
    at_zero = lane % 64 == 0
    number = (lane % 64).astype(F32)
    bd = bd_ref[...]
    bd = bd - bd[:, 0:1]
    bd = jnp.concatenate([bd, bd], axis=1)
    for k in range(4):
        for w in range(4):
            tile, front, back = [], [], []
            for ih in range(2):
                i = k * 32 + ih * 16 + w
                a = jnp.broadcast_to(turned[0:16, i : i + 1], (16, 128))
                b = jnp.broadcast_to(turned[16:32, i : i + 1], (16, 128))
                n = (k * 8 + ih * 4 + w) * 16
                p = proj[n : n + 16]
                proj_ref[ih, 0, k, w] = jnp.where(at_zero, jnp.where(left, a, b), p)
                tile.append(p)
                front.append(a)
                back.append(b)
            own_ref[k, 0, w, 0:16] = jnp.where(left, tile[0], pltpu.roll(tile[1], 64, 1)) + bd
            own_ref[k, 0, w, 16:32] = jnp.where(left, pltpu.roll(tile[0], 64, 1), tile[1]) + bd
            hit = [
                jnp.where(number == jnp.where(left, t[0], t[1]), 1.0, 0.0) for t in (front, back)
            ]
            hits_ref[k, 0, w] = jnp.concatenate(hit, axis=0).astype(BF16)


def bias_kernel(mid_ref, wb_ref, bias_ref, w3_ref, n_ref):
    @pl.when(pl.program_id(0) == 0)
    def _():
        w = jnp.concatenate([wb_ref[...]] * 8, axis=0).T
        lane = lanes_of((128, 128))
        for k in range(8):
            hi, lo = halves(jnp.where(lane // 16 == k, w, 0.0))
            row = jnp.concatenate([hi, lo], axis=1)
            w3_ref[k] = jnp.concatenate([row, row], axis=0)

    n_ref[...] = norm(mid_ref[...])
    acc = jnp.zeros((256, 256), F32)
    for k in range(8):
        x = jnp.concatenate(
            [n_ref[pl.ds(g * 8 + k, 64, stride=32), :] for g in range(4)], axis=0
        )
        hi, lo = halves(x)
        acc = acc + mm(jnp.concatenate([hi, lo], axis=1), w3_ref[k])
    acc = acc[:, :128] + acc[:, 128:]
    for g in range(4):
        bias_ref[:, g * 128 : (g + 1) * 128] = acc[g * 64 : (g + 1) * 64]


def pick_matrix():
    row = lax.broadcasted_iota(jnp.int32, (128, 128), 0)
    return jnp.where((row // 64 == lanes_of((128, 128)) // 64) & (row % 64 == 0), 1.0, 0.0).astype(BF16)


def attention_kernel(
    xr_ref,
    xc_ref,
    bias_ref,
    wq_ref,
    wk_ref,
    wv_ref,
    single_ref,
    wg_ref,
    msg_ref,
    rowpad_ref,
    colpad_ref,
    gate_ref,
):
    gate_ref[...] = 1.0 / (1.0 + jnp.exp(-mm3(norm(single_ref[...]), wg_ref[...])))

    def tokens(ref, n):
        x = jnp.concatenate([ref[pl.ds(q, n, stride=4), :] for q in range(3)], axis=1)
        return norm(x), ref[pl.ds(3, n, stride=4), :][:, 0:1]

    rows, row_pad = tokens(xr_ref, 128)
    cols, col_pad = tokens(xc_ref, 32)
    lane = lanes_of((16, 128))
    for m in range(4):
        a = row_pad[m * 32 : m * 32 + 16]
        b = row_pad[m * 32 + 16 : m * 32 + 32]
        rowpad_ref[m * 16 : (m + 1) * 16, :] = jnp.where(lane < 64, a, b)
    colpad_ref[...] = jnp.broadcast_to(col_pad, (32, 128))
    query = mm3(rows, wq_ref[...]) * (24.0**-0.5)
    key = mm3(cols, wk_ref[...])
    value = mm3(cols, wv_ref[...])
    of_head = lanes_of((16, 384)) // 24 == lax.broadcasted_iota(jnp.int32, (16, 384), 0)

    def spread(y):
        return jnp.where(of_head[None], y[:, None, :], 0.0).reshape(512, 384)

    scores = mm3(query, spread(key), mm_nt) + bias_ref[...]
    of_key = lanes_of((32, 512)) // 16 == lax.broadcasted_iota(jnp.int32, (32, 512), 0)
    pad_lane = jnp.sum(jnp.where(of_key, col_pad, 0.0), axis=0, keepdims=True)
    scores = jnp.where(pad_lane > 0.5, scores, -1000000000.0)

    def over_keys(y, op):
        r = op(op(y[:, :128], y[:, 128:256]), op(y[:, 256:384], y[:, 384:]))
        for shift in (16, 32, 64):
            r = op(r, pltpu.roll(r, shift, 1))
        return r

    top = over_keys(scores, jnp.maximum)
    expo = jnp.exp(scores - jnp.concatenate([top] * 4, axis=1))
    total = over_keys(expo, jnp.add)
    acc = mm3(expo, spread(value))
    lane = lanes_of((128, 128))
    tail = jnp.where(lane < 16, total, jnp.where(lane < 32, top, 0.0))
    for q in range(3):
        msg_ref[pl.ds(q, 128, stride=4), :] = acc[:, q * 128 : (q + 1) * 128]
    msg_ref[pl.ds(3, 128, stride=4), :] = tail


def merge_kernel(msg_ref, single_ref, gate_ref, wo_ref, out_ref):
    lane = lanes_of((32, 128))
    accs, factors, totals = [], [], []
    for t in range(4):
        part = [msg_ref[pl.ds(4 * t + q, 32, stride=16), :] for q in range(4)]
        accs.append(jnp.concatenate(part[:3], axis=1))
        tail = part[3]
        local = pltpu.roll(tail, 112, 1)
        top = jnp.max(local, axis=0, keepdims=True)
        f = jnp.where(lane < 16, jnp.exp(local - top), 0.0)
        factors.append(f)
        totals.append(jnp.sum(f * tail, axis=0, keepdims=True))
    expand = jnp.where(
        lanes_of((128, 384)) // 24 == lax.broadcasted_iota(jnp.int32, (128, 384), 0), 1.0, 0.0
    )
    stacked = jnp.concatenate(factors + totals + totals, axis=0)
    wide = jnp.dot(stacked, expand, precision=lax.Precision.HIGHEST, preferred_element_type=F32)
    rows = []
    for t in range(4):
        num = jnp.sum(wide[t * 32 : (t + 1) * 32] * accs[t], axis=0, keepdims=True)
        rows.append(num / wide[128 + t : 129 + t])
    attended = jnp.concatenate(rows, axis=0)
    out_ref[...] = single_ref[...] + mm3(gate_ref[...] * attended, wo_ref[...])


def gradient_kernel(place_ref, *refs):
    parts = refs[:8]
    own_ref, hits_ref, mid_ref, rowpad_ref, colpad_ref, wdt_ref, out_ref = refs[8:15]
    f_ref, w_ref, ones_ref, pick_ref, d_ref = refs[15:]

    @pl.when(pl.program_id(0) == 0)
    def _():
        d = wdt_ref[...]
        z = jnp.zeros_like(d)
        both = jnp.concatenate(
            [jnp.concatenate([d, z], axis=1), jnp.concatenate([z, d], axis=1)], axis=0
        )
        hi, lo = halves(both)
        w_ref[0] = jnp.concatenate([hi, hi], axis=0)
        w_ref[1] = jnp.concatenate([lo, lo], axis=0)
        row = lax.broadcasted_iota(jnp.int32, (256, 128), 0) % 128
        same = row // 64 == lanes_of((256, 128)) // 64
        ones_ref[...] = jnp.where(same, 1.0, 0.0).astype(BF16)
        pick_ref[...] = pick_matrix()

    for p in range(8):
        place = place_ref[0] ^ p
        f_ref[pl.ds(pl.multiple_of(place * 64, 64), 64), :] = parts[p][0]

    lane = lanes_of((512, 128))
    first = lane < 64
    bins = lane % 64
    flip = jnp.concatenate([f_ref[pl.ds(i, 32, stride=16), :] for i in range(16)], axis=0)
    mark = jnp.where(bins == 0, flip, 0.0)
    target = mm(mark.astype(BF16), pick_ref[...])
    logits = own_ref[...].reshape(512, 128) + (flip - mark)
    top_a = jnp.max(jnp.where(first, logits, -3.0e38), axis=-1, keepdims=True)
    top_b = jnp.max(jnp.where(first, -3.0e38, logits), axis=-1, keepdims=True)
    expo = jnp.exp(logits - jnp.where(first, top_a, top_b))
    hi, lo = halves(expo)
    total = mm(jnp.concatenate([hi, lo], axis=1), ones_ref[...])
    hits = jnp.where(bins.astype(F32) == target, 1.0, 0.0) + hits_ref[...].reshape(512, 128).astype(F32)
    mask = rowpad_ref[...][:, None, :] * colpad_ref[...][None]
    hi, lo = halves(mask.reshape(512, 128) * (expo * (2.0 / total) - hits))
    d_ref[...] = jnp.concatenate([hi, lo], axis=1)
    change = mm(d_ref[...], w_ref[0]) + mm(d_ref[...], w_ref[1])
    for k in range(2):
        out_ref[0, k] = mid_ref[0, k] + change[:, k * 128 : (k + 1) * 128].reshape(16, 32, 128)


def tokens_kernel(single_ref, pad_ref, out_ref):
    tile = []
    for t in range(4):
        for q in range(3):
            tile.append(single_ref[t : t + 1, q * 128 : (q + 1) * 128])
        tile.append(jnp.full((1, 128), pad_ref[t].astype(F32)))
    out_ref[...] = jnp.broadcast_to(jnp.concatenate(tile, axis=0)[None], (32, 16, 128))


def full(shape):
    return pl.BlockSpec(shape, lambda *_: (0,) * len(shape))


def struct(*shape):
    return jax.ShapeDtypeStruct(shape, F32)


def per_device(
    pair,
    single,
    target_bins,
    token_pad,
    w_gate,
    w_up,
    w_out,
    w_bias,
    w_query,
    w_key,
    w_value,
    w_gating,
    w_attn_out,
    w_dist,
    b_dist,
):
    at = {name: lax.axis_index(name) for name in ALL}
    coords = all_coords()
    tt = target_bins.T
    wdt = w_dist.T

    tok = pl.pallas_call(
        tokens_kernel,
        in_specs=[full((4, 384)), pl.BlockSpec(memory_space=pltpu.SMEM)],
        out_shape=struct(32, 16, 128),
        name="tokens",
    )(single, token_pad)
    rows_tok = lax.all_to_all(tok, COL, split_axis=0, concat_axis=0, tiled=True)
    rows_tok = rows_tok.reshape(512, 128)

    mid, proj, own, hits = pl.pallas_call(
        transition_kernel,
        grid=(4,),
        in_specs=[
            pl.BlockSpec((4, 2, 1, 4, 32, 128), lambda s: (0, 0, s, 0, 0, 0)),
            full((32, 128)),
            full((128, 512)),
            full((128, 512)),
            full((512, 128)),
            full((64, 128)),
            full((1, 64)),
        ],
        out_specs=[
            pl.BlockSpec((4, 2, 1, 4, 32, 128), lambda s: (0, 0, s, 0, 0, 0)),
            pl.BlockSpec((2, 1, 4, 4, 16, 128), lambda s: (0, s, 0, 0, 0, 0)),
            pl.BlockSpec((4, 1, 4, 32, 128), lambda s: (0, s, 0, 0, 0)),
            pl.BlockSpec((4, 1, 4, 32, 128), lambda s: (0, s, 0, 0, 0)),
        ],
        out_shape=[
            struct(4, 2, 4, 4, 32, 128),
            struct(2, 4, 4, 4, 16, 128),
            struct(4, 4, 4, 32, 128),
            jax.ShapeDtypeStruct((4, 4, 4, 32, 128), BF16),
        ],
        scratch_shapes=[
            pltpu.VMEM((2, 2, 256, 512), BF16),
            pltpu.VMEM((512, 256), BF16),
            pltpu.VMEM((256, 256), BF16),
        ],
        name="transition",
    )(pair.reshape(4, 2, 4, 4, 32, 128), tt, w_gate, w_up, w_out, wdt, b_dist[None])

    spread = lax.all_to_all(
        proj.reshape(32, 64, 128), PLANE, split_axis=0, concat_axis=0, tiled=True
    )
    spread = spread.reshape(8, 4, 64, 128)

    quarter = lax.dynamic_slice_in_dim(rows_tok, (at["yl"] * 2 + at["core"]) * 128, 128, 0)
    perm = [
        (flat_index(c), flat_index((c[2], c[3] ^ c[1], c[0], c[1], c[4], c[5]))) for c in coords
    ]
    cols_tok = lax.ppermute(quarter, ALL, perm)

    bias = pl.pallas_call(
        bias_kernel,
        grid=(2,),
        in_specs=[pl.BlockSpec((2048, 128), lambda m: (m, 0)), full((16, 128))],
        out_specs=pl.BlockSpec((64, 512), lambda m: (m, 0)),
        out_shape=struct(128, 512),
        scratch_shapes=[pltpu.VMEM((8, 256, 256), BF16), pltpu.VMEM((2048, 128), F32)],
        name="bias",
    )(mid.reshape(4096, 128), w_bias.T)

    msg, rowpad, colpad, gate = pl.pallas_call(
        attention_kernel,
        out_shape=[struct(512, 128), struct(64, 128), struct(32, 128), struct(4, 384)],
        name="attention",
    )(rows_tok, cols_tok, bias, w_query, w_key, w_value, single, w_gating)

    parts = []
    for n in range(8):
        u, v = n // 2, n % 2
        piece = lax.dynamic_index_in_dim(
            spread, (at["x"] ^ u) * 2 + (at["yh"] ^ v), 0, keepdims=False
        )
        perm = []
        for c in coords:
            x, zh, zl, yh, yl, core = c
            perm.append((flat_index(c), flat_index((zl, yh ^ v, x ^ u, zh, yl, core))))
        parts.append(lax.ppermute(piece, ALL, perm))
    place = (at["zl"] * 2 + at["zh"]).reshape(1)

    merged = lax.all_to_all(msg.reshape(32, 16, 128), COL, split_axis=0, concat_axis=0, tiled=True)
    merged = merged.reshape(512, 128)
    single_out = pl.pallas_call(merge_kernel, out_shape=struct(4, 384), name="merge")(
        merged, single, gate, w_attn_out
    )
    grouped = pl.BlockSpec((1, 2, 16, 32, 128), lambda m, _: (m, 0, 0, 0, 0))
    pair_out = pl.pallas_call(
        gradient_kernel,
        grid_spec=pltpu.PrefetchScalarGridSpec(
            num_scalar_prefetch=1,
            grid=(4,),
            in_specs=[pl.BlockSpec((1, 64, 128), lambda m, _: (m, 0, 0))] * 8
            + [
                pl.BlockSpec((16, 32, 128), lambda m, _: (m, 0, 0)),
                pl.BlockSpec((16, 32, 128), lambda m, _: (m, 0, 0)),
                grouped,
                pl.BlockSpec((16, 128), lambda m, _: (m, 0)),
                full((32, 128)),
                full((64, 128)),
            ],
            out_specs=grouped,
            scratch_shapes=[
                pltpu.VMEM((512, 128), F32),
                pltpu.VMEM((2, 256, 256), BF16),
                pltpu.VMEM((256, 128), BF16),
                pltpu.VMEM((128, 128), BF16),
                pltpu.VMEM((512, 256), BF16),
            ],
        ),
        out_shape=struct(4, 2, 16, 32, 128),
        name="gradient",
    )(
        place,
        *parts,
        own.reshape(64, 32, 128),
        hits.reshape(64, 32, 128),
        mid.reshape(4, 2, 16, 32, 128),
        rowpad,
        colpad,
        wdt,
    )
    pair_out = pair_out.reshape(128, 32, 128)
    return (pair_out, single_out)


def solution(mesh):
    fine = Mesh(mesh.devices.reshape(SIZES), ALL)
    row, col = ("x", "zh"), COL
    in_specs = (
        P(row, col, None),
        P(ALL, None),
        P(row, col),
        P(ALL),
    ) + (P(),) * 11
    out_specs = (P(row, col, None), P(ALL, None))
    return jax.shard_map(
        per_device, mesh=fine, in_specs=in_specs, out_specs=out_specs, check_vma=False
    )
```

```python
import jax
import jax.numpy as jnp
from jax import lax
from jax.experimental import pallas as pl
from jax.experimental.pallas import tpu as pltpu
from jax.sharding import Mesh, PartitionSpec as P


F32 = jnp.float32
BF16 = jnp.bfloat16
ALL = ("x", "zh", "zl", "yh", "yl", "core")
COL = ("zl", "yh", "yl", "core")
PLANE = ("x", "yh", "yl", "core")
SIZES = (4, 2, 4, 2, 2, 2)


def flat_index(coords):
    index = 0
    for c, n in zip(coords, SIZES):
        index = index * n + c
    return index


def all_coords():
    out = [()]
    for n in SIZES:
        out = [c + (k,) for c in out for k in range(n)]
    return out


def halves(x):
    hi = x.astype(BF16)
    lo = (x - hi.astype(F32)).astype(BF16)
    return hi, lo


def mm(a, b):
    return jnp.dot(a, b, preferred_element_type=F32)


def mm_nt(a, b):
    return lax.dot_general(a, b, (((1,), (1,)), ((), ())), preferred_element_type=F32)


def mm3(a, b, dot=mm):
    ah, al = halves(a)
    bh, bl = halves(b)
    return dot(ah, bh) + (dot(al, bh) + dot(ah, bl))


def norm(x):
    mean = jnp.mean(x, axis=-1, keepdims=True)
    centred = x - mean
    var = jnp.mean(centred * centred, axis=-1, keepdims=True)
    return centred * lax.rsqrt(var + 1e-05)


def lanes_of(shape):
    return lax.broadcasted_iota(jnp.int32, shape, len(shape) - 1)


def doubled_projection(wdt_ref):
    d = wdt_ref[...]
    d = d - d[0:1, :]
    z = jnp.zeros_like(d)
    both = jnp.concatenate(
        [jnp.concatenate([d, z], axis=1), jnp.concatenate([z, d], axis=1)], axis=0
    )
    hi, lo = halves(both.T)
    return jnp.concatenate([hi, lo], axis=1)


def project(a, b, wp_ref):
    xh, xl = halves(jnp.concatenate([a, b], axis=1))
    p = mm(xh, wp_ref[...])
    return p[:, :128] + (p[:, 128:] + mm(xl, wp_ref[:, :128]))


def transition_kernel(
    pair_ref,
    tt_ref,
    wg_ref,
    wu_ref,
    wo_ref,
    wdt_ref,
    bd_ref,
    mid_ref,
    proj_ref,
    own_ref,
    hits_ref,
    w1_ref,
    w2_ref,
    wp_ref,
):
    step = pl.program_id(0)

    @pl.when(step == 0)
    def _():
        for k, ref in enumerate((wg_ref, wu_ref)):
            hi, lo = halves(ref[...])
            w1_ref[k, 0] = jnp.concatenate([hi, hi], axis=0)
            w1_ref[k, 1] = jnp.concatenate([lo, lo], axis=0)
        hi, lo = halves(wo_ref[...])
        w2_ref[...] = jnp.concatenate([hi, lo], axis=1)
        wp_ref[...] = doubled_projection(wdt_ref)

    x = pair_ref[...].reshape(1024, 128)
    nh, nl = halves(norm(x))
    both = jnp.concatenate([nh, nl], axis=1)
    out = jnp.zeros((1024, 128), F32)
    for c in range(0, 512, 256):
        gate = mm(both, w1_ref[0, 0, :, c : c + 256]) + mm(both, w1_ref[0, 1, :, c : c + 256])
        up = mm(both, w1_ref[1, 0, :, c : c + 256]) + mm(both, w1_ref[1, 1, :, c : c + 256])
        hidden = gate / (1.0 + jnp.exp(-gate)) * up
        hh, hl = halves(hidden)
        o = mm(hh, w2_ref[c : c + 256, :])
        out = out + (o[:, :128] + (o[:, 128:] + mm(hl, w2_ref[c : c + 256, :128])))
    mid = x + out
    mid_ref[...] = mid.reshape(4, 2, 1, 4, 32, 128)
    split = mid.reshape(32, 2, 16, 128)
    proj = project(split[:, 0].reshape(512, 128), split[:, 1].reshape(512, 128), wp_ref)
    turned = pltpu.roll(tt_ref[...].astype(F32), (128 - 4 * step) % 128, 1)
    lane = lanes_of((16, 128))
    left = lane < 64
    at_zero = lane % 64 == 0
    number = (lane % 64).astype(F32)
    bd = bd_ref[...]
    bd = bd - bd[:, 0:1]
    bd = jnp.concatenate([bd, bd], axis=1)
    for k in range(4):
        for w in range(4):
            tile, front, back = [], [], []
            for ih in range(2):
                i = k * 32 + ih * 16 + w
                a = jnp.broadcast_to(turned[0:16, i : i + 1], (16, 128))
                b = jnp.broadcast_to(turned[16:32, i : i + 1], (16, 128))
                n = (k * 8 + ih * 4 + w) * 16
                p = proj[n : n + 16]
                proj_ref[ih, 0, k, w] = jnp.where(at_zero, jnp.where(left, a, b), p)
                tile.append(p)
                front.append(a)
                back.append(b)
            own_ref[k, 0, w, 0:16] = jnp.where(left, tile[0], pltpu.roll(tile[1], 64, 1)) + bd
            own_ref[k, 0, w, 16:32] = jnp.where(left, pltpu.roll(tile[0], 64, 1), tile[1]) + bd
            hit = [
                jnp.where(number == jnp.where(left, t[0], t[1]), 1.0, 0.0) for t in (front, back)
            ]
            hits_ref[k, 0, w] = jnp.concatenate(hit, axis=0).astype(BF16)


def bias_kernel(mid_ref, wb_ref, bias_ref, w3_ref, n_ref):
    @pl.when(pl.program_id(0) == 0)
    def _():
        w = jnp.concatenate([wb_ref[...]] * 8, axis=0).T
        lane = lanes_of((128, 128))
        for k in range(8):
            hi, lo = halves(jnp.where(lane // 16 == k, w, 0.0))
            row = jnp.concatenate([hi, lo], axis=1)
            w3_ref[k] = jnp.concatenate([row, row], axis=0)

    n_ref[...] = norm(mid_ref[...])
    acc = jnp.zeros((256, 256), F32)
    for k in range(8):
        x = jnp.concatenate(
            [n_ref[pl.ds(g * 8 + k, 64, stride=32), :] for g in range(4)], axis=0
        )
        hi, lo = halves(x)
        acc = acc + mm(jnp.concatenate([hi, lo], axis=1), w3_ref[k])
    acc = acc[:, :128] + acc[:, 128:]
    for g in range(4):
        bias_ref[:, g * 128 : (g + 1) * 128] = acc[g * 64 : (g + 1) * 64]


def pick_matrix():
    row = lax.broadcasted_iota(jnp.int32, (128, 128), 0)
    return jnp.where((row // 64 == lanes_of((128, 128)) // 64) & (row % 64 == 0), 1.0, 0.0).astype(BF16)


def attention_kernel(
    xr_ref,
    xc_ref,
    bias_ref,
    wq_ref,
    wk_ref,
    wv_ref,
    single_ref,
    wg_ref,
    msg_ref,
    rowpad_ref,
    colpad_ref,
    gate_ref,
):
    gate_ref[...] = 1.0 / (1.0 + jnp.exp(-mm3(norm(single_ref[...]), wg_ref[...])))

    def tokens(ref, n):
        x = jnp.concatenate([ref[pl.ds(q, n, stride=4), :] for q in range(3)], axis=1)
        return norm(x), ref[pl.ds(3, n, stride=4), :][:, 0:1]

    rows, row_pad = tokens(xr_ref, 128)
    cols, col_pad = tokens(xc_ref, 32)
    lane = lanes_of((16, 128))
    for m in range(4):
        a = row_pad[m * 32 : m * 32 + 16]
        b = row_pad[m * 32 + 16 : m * 32 + 32]
        rowpad_ref[m * 16 : (m + 1) * 16, :] = jnp.where(lane < 64, a, b)
    colpad_ref[...] = jnp.broadcast_to(col_pad, (32, 128))
    query = mm3(rows, wq_ref[...]) * (24.0**-0.5)
    key = mm3(cols, wk_ref[...])
    value = mm3(cols, wv_ref[...])
    of_head = lanes_of((16, 384)) // 24 == lax.broadcasted_iota(jnp.int32, (16, 384), 0)

    def spread(y):
        return jnp.where(of_head[None], y[:, None, :], 0.0).reshape(512, 384)

    scores = mm3(query, spread(key), mm_nt) + bias_ref[...]
    of_key = lanes_of((32, 512)) // 16 == lax.broadcasted_iota(jnp.int32, (32, 512), 0)
    pad_lane = jnp.sum(jnp.where(of_key, col_pad, 0.0), axis=0, keepdims=True)
    scores = jnp.where(pad_lane > 0.5, scores, -1000000000.0)

    def over_keys(y, op):
        r = op(op(y[:, :128], y[:, 128:256]), op(y[:, 256:384], y[:, 384:]))
        for shift in (16, 32, 64):
            r = op(r, pltpu.roll(r, shift, 1))
        return r

    top = over_keys(scores, jnp.maximum)
    expo = jnp.exp(scores - jnp.concatenate([top] * 4, axis=1))
    total = over_keys(expo, jnp.add)
    acc = mm3(expo, spread(value))
    lane = lanes_of((128, 128))
    tail = jnp.where(lane < 16, total, jnp.where(lane < 32, top, 0.0))
    for q in range(3):
        msg_ref[pl.ds(q, 128, stride=4), :] = acc[:, q * 128 : (q + 1) * 128]
    msg_ref[pl.ds(3, 128, stride=4), :] = tail


def merge_kernel(msg_ref, single_ref, gate_ref, wo_ref, out_ref):
    lane = lanes_of((32, 128))
    accs, factors, totals = [], [], []
    for t in range(4):
        part = [msg_ref[pl.ds(4 * t + q, 32, stride=16), :] for q in range(4)]
        accs.append(jnp.concatenate(part[:3], axis=1))
        tail = part[3]
        local = pltpu.roll(tail, 112, 1)
        top = jnp.max(local, axis=0, keepdims=True)
        f = jnp.where(lane < 16, jnp.exp(local - top), 0.0)
        factors.append(f)
        totals.append(jnp.sum(f * tail, axis=0, keepdims=True))
    expand = jnp.where(
        lanes_of((128, 384)) // 24 == lax.broadcasted_iota(jnp.int32, (128, 384), 0), 1.0, 0.0
    )
    stacked = jnp.concatenate(factors + totals + totals, axis=0)
    wide = jnp.dot(stacked, expand, precision=lax.Precision.HIGHEST, preferred_element_type=F32)
    rows = []
    for t in range(4):
        num = jnp.sum(wide[t * 32 : (t + 1) * 32] * accs[t], axis=0, keepdims=True)
        rows.append(num / wide[128 + t : 129 + t])
    attended = jnp.concatenate(rows, axis=0)
    out_ref[...] = single_ref[...] + mm3(gate_ref[...] * attended, wo_ref[...])


def gradient_kernel(place_ref, *refs):
    parts = refs[:8]
    own_ref, hits_ref, mid_ref, rowpad_ref, colpad_ref, wdt_ref, out_ref = refs[8:15]
    f_ref, w_ref, ones_ref, pick_ref, d_ref = refs[15:]

    @pl.when(pl.program_id(0) == 0)
    def _():
        d = wdt_ref[...]
        z = jnp.zeros_like(d)
        both = jnp.concatenate(
            [jnp.concatenate([d, z], axis=1), jnp.concatenate([z, d], axis=1)], axis=0
        )
        hi, lo = halves(both)
        w_ref[0] = jnp.concatenate([hi, hi], axis=0)
        w_ref[1] = jnp.concatenate([lo, lo], axis=0)
        row = lax.broadcasted_iota(jnp.int32, (256, 128), 0) % 128
        same = row // 64 == lanes_of((256, 128)) // 64
        ones_ref[...] = jnp.where(same, 1.0, 0.0).astype(BF16)
        pick_ref[...] = pick_matrix()

    for p in range(8):
        place = place_ref[0] ^ p
        f_ref[pl.ds(pl.multiple_of(place * 64, 64), 64), :] = parts[p][pl.program_id(0)]

    lane = lanes_of((512, 128))
    first = lane < 64
    bins = lane % 64
    flip = jnp.concatenate([f_ref[pl.ds(i, 32, stride=16), :] for i in range(16)], axis=0)
    mark = jnp.where(bins == 0, flip, 0.0)
    target = mm(mark.astype(BF16), pick_ref[...])
    logits = own_ref[...].reshape(512, 128) + (flip - mark)
    top_a = jnp.max(jnp.where(first, logits, -3.0e38), axis=-1, keepdims=True)
    top_b = jnp.max(jnp.where(first, -3.0e38, logits), axis=-1, keepdims=True)
    expo = jnp.exp(logits - jnp.where(first, top_a, top_b))
    hi, lo = halves(expo)
    total = mm(jnp.concatenate([hi, lo], axis=1), ones_ref[...])
    hits = jnp.where(bins.astype(F32) == target, 1.0, 0.0) + hits_ref[...].reshape(512, 128).astype(F32)
    mask = rowpad_ref[...][:, None, :] * colpad_ref[...][None]
    hi, lo = halves(mask.reshape(512, 128) * (expo * (2.0 / total) - hits))
    d_ref[...] = jnp.concatenate([hi, lo], axis=1)
    change = mm(d_ref[...], w_ref[0]) + mm(d_ref[...], w_ref[1])
    for k in range(2):
        out_ref[0, k] = mid_ref[0, k] + change[:, k * 128 : (k + 1) * 128].reshape(16, 32, 128)


def tokens_kernel(single_ref, pad_ref, out_ref):
    tile = []
    for t in range(4):
        for q in range(3):
            tile.append(single_ref[t : t + 1, q * 128 : (q + 1) * 128])
        tile.append(jnp.full((1, 128), pad_ref[t].astype(F32)))
    out_ref[...] = jnp.broadcast_to(jnp.concatenate(tile, axis=0)[None], (32, 16, 128))


def full(shape):
    return pl.BlockSpec(shape, lambda *_: (0,) * len(shape))


def near(x):
    return pltpu.with_memory_space_constraint(x, pltpu.VMEM)


def struct(*shape):
    return jax.ShapeDtypeStruct(shape, F32)


def per_device(
    pair,
    single,
    target_bins,
    token_pad,
    w_gate,
    w_up,
    w_out,
    w_bias,
    w_query,
    w_key,
    w_value,
    w_gating,
    w_attn_out,
    w_dist,
    b_dist,
):
    at = {name: lax.axis_index(name) for name in ALL}
    coords = all_coords()
    tt = target_bins.T
    wdt = w_dist.T

    tok = pl.pallas_call(
        tokens_kernel,
        in_specs=[full((4, 384)), pl.BlockSpec(memory_space=pltpu.SMEM)],
        out_shape=struct(32, 16, 128),
        name="tokens",
    )(single, token_pad)
    rows_tok = lax.all_to_all(tok, COL, split_axis=0, concat_axis=0, tiled=True)
    rows_tok = rows_tok.reshape(512, 128)

    mid, proj, own, hits = pl.pallas_call(
        transition_kernel,
        grid=(4,),
        in_specs=[
            pl.BlockSpec((4, 2, 1, 4, 32, 128), lambda s: (0, 0, s, 0, 0, 0)),
            full((32, 128)),
            full((128, 512)),
            full((128, 512)),
            full((512, 128)),
            full((64, 128)),
            full((1, 64)),
        ],
        out_specs=[
            pl.BlockSpec((4, 2, 1, 4, 32, 128), lambda s: (0, 0, s, 0, 0, 0)),
            pl.BlockSpec((2, 1, 4, 4, 16, 128), lambda s: (0, s, 0, 0, 0, 0)),
            pl.BlockSpec((4, 1, 4, 32, 128), lambda s: (0, s, 0, 0, 0)),
            pl.BlockSpec((4, 1, 4, 32, 128), lambda s: (0, s, 0, 0, 0)),
        ],
        out_shape=[
            struct(4, 2, 4, 4, 32, 128),
            struct(2, 4, 4, 4, 16, 128),
            struct(4, 4, 4, 32, 128),
            jax.ShapeDtypeStruct((4, 4, 4, 32, 128), BF16),
        ],
        scratch_shapes=[
            pltpu.VMEM((2, 2, 256, 512), BF16),
            pltpu.VMEM((512, 256), BF16),
            pltpu.VMEM((256, 256), BF16),
        ],
        name="transition",
    )(pair.reshape(4, 2, 4, 4, 32, 128), tt, w_gate, w_up, w_out, wdt, b_dist[None])

    spread = lax.all_to_all(
        proj.reshape(32, 64, 128), PLANE, split_axis=0, concat_axis=0, tiled=True
    )
    spread = spread.reshape(8, 4, 64, 128)

    quarter = lax.dynamic_slice_in_dim(rows_tok, (at["yl"] * 2 + at["core"]) * 128, 128, 0)
    perm = [
        (flat_index(c), flat_index((c[2], c[3] ^ c[1], c[0], c[1], c[4], c[5]))) for c in coords
    ]
    cols_tok = lax.ppermute(quarter, ALL, perm)

    bias = pl.pallas_call(
        bias_kernel,
        grid=(2,),
        in_specs=[pl.BlockSpec((2048, 128), lambda m: (m, 0)), full((16, 128))],
        out_specs=pl.BlockSpec((64, 512), lambda m: (m, 0)),
        out_shape=struct(128, 512),
        scratch_shapes=[pltpu.VMEM((8, 256, 256), BF16), pltpu.VMEM((2048, 128), F32)],
        name="bias",
    )(mid.reshape(4096, 128), w_bias.T)

    msg, rowpad, colpad, gate = pl.pallas_call(
        attention_kernel,
        in_specs=[pl.BlockSpec(memory_space=pltpu.VMEM)] * 8,
        out_shape=[struct(512, 128), struct(64, 128), struct(32, 128), struct(4, 384)],
        name="attention",
    )(near(rows_tok), near(cols_tok), bias, w_query, w_key, w_value, single, w_gating)

    parts = []
    for n in range(8):
        u, v = n // 2, n % 2
        piece = lax.dynamic_index_in_dim(
            spread, (at["x"] ^ u) * 2 + (at["yh"] ^ v), 0, keepdims=False
        )
        perm = []
        for c in coords:
            x, zh, zl, yh, yl, core = c
            perm.append((flat_index(c), flat_index((zl, yh ^ v, x ^ u, zh, yl, core))))
        parts.append(lax.ppermute(piece, ALL, perm))
    place = (at["zl"] * 2 + at["zh"]).reshape(1)

    merged = lax.all_to_all(msg.reshape(32, 16, 128), COL, split_axis=0, concat_axis=0, tiled=True)
    merged = merged.reshape(512, 128)
    single_out = pl.pallas_call(
        merge_kernel,
        in_specs=[pl.BlockSpec(memory_space=pltpu.VMEM)] * 4,
        out_shape=struct(4, 384),
        name="merge",
    )(
        near(merged), single, gate, w_attn_out
    )
    grouped = pl.BlockSpec((1, 2, 16, 32, 128), lambda m, _: (m, 0, 0, 0, 0))
    pair_out = pl.pallas_call(
        gradient_kernel,
        grid_spec=pltpu.PrefetchScalarGridSpec(
            num_scalar_prefetch=1,
            grid=(4,),
            in_specs=[pl.BlockSpec(memory_space=pltpu.VMEM)] * 8
            + [
                pl.BlockSpec((16, 32, 128), lambda m, _: (m, 0, 0)),
                pl.BlockSpec((16, 32, 128), lambda m, _: (m, 0, 0)),
                grouped,
                pl.BlockSpec((16, 128), lambda m, _: (m, 0)),
                full((32, 128)),
                full((64, 128)),
            ],
            out_specs=grouped,
            scratch_shapes=[
                pltpu.VMEM((512, 128), F32),
                pltpu.VMEM((2, 256, 256), BF16),
                pltpu.VMEM((256, 128), BF16),
                pltpu.VMEM((128, 128), BF16),
                pltpu.VMEM((512, 256), BF16),
            ],
        ),
        out_shape=struct(4, 2, 16, 32, 128),
        name="gradient",
    )(
        place,
        *(near(p) for p in parts),
        own.reshape(64, 32, 128),
        hits.reshape(64, 32, 128),
        mid.reshape(4, 2, 16, 32, 128),
        rowpad,
        colpad,
        wdt,
    )
    pair_out = pair_out.reshape(128, 32, 128)
    return (pair_out, single_out)


def solution(mesh):
    fine = Mesh(mesh.devices.reshape(SIZES), ALL)
    row, col = ("x", "zh"), COL
    in_specs = (
        P(row, col, None),
        P(ALL, None),
        P(row, col),
        P(ALL),
    ) + (P(),) * 11
    out_specs = (P(row, col, None), P(ALL, None))
    return jax.shard_map(
        per_device, mesh=fine, in_specs=in_specs, out_specs=out_specs, check_vma=False
    )
```

```python
import jax
import jax.numpy as jnp
from jax import lax
from jax.experimental import pallas as pl
from jax.experimental.pallas import tpu as pltpu
from jax.sharding import Mesh, PartitionSpec as P


F32 = jnp.float32
BF16 = jnp.bfloat16
ALL = ("x", "zh", "zl", "yh", "yl", "core")
COL = ("zl", "yh", "yl", "core")
PLANE = ("x", "yh", "yl", "core")
SIZES = (4, 2, 4, 2, 2, 2)


def flat_index(coords):
    index = 0
    for c, n in zip(coords, SIZES):
        index = index * n + c
    return index


def all_coords():
    out = [()]
    for n in SIZES:
        out = [c + (k,) for c in out for k in range(n)]
    return out


def halves(x):
    hi = x.astype(BF16)
    lo = (x - hi.astype(F32)).astype(BF16)
    return hi, lo


def mm(a, b):
    return jnp.dot(a, b, preferred_element_type=F32)


def mm_nt(a, b):
    return lax.dot_general(a, b, (((1,), (1,)), ((), ())), preferred_element_type=F32)


def mm3(a, b, dot=mm):
    ah, al = halves(a)
    bh, bl = halves(b)
    return dot(ah, bh) + (dot(al, bh) + dot(ah, bl))


def norm(x):
    mean = jnp.mean(x, axis=-1, keepdims=True)
    centred = x - mean
    var = jnp.mean(centred * centred, axis=-1, keepdims=True)
    return centred * lax.rsqrt(var + 1e-05)


def lanes_of(shape):
    return lax.broadcasted_iota(jnp.int32, shape, len(shape) - 1)


def doubled_projection(wdt_ref):
    d = wdt_ref[...]
    d = d - d[0:1, :]
    z = jnp.zeros_like(d)
    both = jnp.concatenate(
        [jnp.concatenate([d, z], axis=1), jnp.concatenate([z, d], axis=1)], axis=0
    )
    hi, lo = halves(both.T)
    return jnp.concatenate([hi, lo], axis=1)


def project(a, b, wp_ref):
    xh, xl = halves(jnp.concatenate([a, b], axis=1))
    p = mm(xh, wp_ref[...])
    return p[:, :128] + (p[:, 128:] + mm(xl, wp_ref[:, :128]))


def transition_kernel(
    pair_ref,
    tt_ref,
    wg_ref,
    wu_ref,
    wo_ref,
    wdt_ref,
    bd_ref,
    mid_ref,
    proj_ref,
    own_ref,
    hits_ref,
    w1_ref,
    w2_ref,
    wp_ref,
):
    step = pl.program_id(0)

    @pl.when(step == 0)
    def _():
        for k, ref in enumerate((wg_ref, wu_ref)):
            hi, lo = halves(ref[...])
            w1_ref[k, 0] = jnp.concatenate([hi, hi], axis=0)
            w1_ref[k, 1] = jnp.concatenate([lo, lo], axis=0)
        hi, lo = halves(wo_ref[...])
        w2_ref[...] = jnp.concatenate([hi, lo], axis=1)
        wp_ref[...] = doubled_projection(wdt_ref)

    x = pair_ref[...].reshape(1024, 128)
    nh, nl = halves(norm(x))
    both = jnp.concatenate([nh, nl], axis=1)
    out = jnp.zeros((1024, 128), F32)
    for c in range(0, 512, 256):
        gate = mm(both, w1_ref[0, 0, :, c : c + 256]) + mm(both, w1_ref[0, 1, :, c : c + 256])
        up = mm(both, w1_ref[1, 0, :, c : c + 256]) + mm(both, w1_ref[1, 1, :, c : c + 256])
        hidden = gate / (1.0 + jnp.exp(-gate)) * up
        hh, hl = halves(hidden)
        o = mm(hh, w2_ref[c : c + 256, :])
        out = out + (o[:, :128] + (o[:, 128:] + mm(hl, w2_ref[c : c + 256, :128])))
    mid = x + out
    mid_ref[...] = mid.reshape(4, 2, 1, 4, 32, 128)
    split = mid.reshape(32, 2, 16, 128)
    proj = project(split[:, 0].reshape(512, 128), split[:, 1].reshape(512, 128), wp_ref)
    turned = pltpu.roll(tt_ref[...].astype(F32), (128 - 4 * step) % 128, 1)
    lane = lanes_of((16, 128))
    left = lane < 64
    at_zero = lane % 64 == 0
    number = (lane % 64).astype(F32)
    bd = bd_ref[...]
    bd = bd - bd[:, 0:1]
    bd = jnp.concatenate([bd, bd], axis=1)
    for k in range(4):
        for w in range(4):
            tile, front, back = [], [], []
            for ih in range(2):
                i = k * 32 + ih * 16 + w
                a = jnp.broadcast_to(turned[0:16, i : i + 1], (16, 128))
                b = jnp.broadcast_to(turned[16:32, i : i + 1], (16, 128))
                n = (k * 8 + ih * 4 + w) * 16
                p = proj[n : n + 16]
                proj_ref[ih, 0, k, w] = jnp.where(at_zero, jnp.where(left, a, b), p)
                tile.append(p)
                front.append(a)
                back.append(b)
            own_ref[k, 0, w, 0:16] = jnp.where(left, tile[0], pltpu.roll(tile[1], 64, 1)) + bd
            own_ref[k, 0, w, 16:32] = jnp.where(left, pltpu.roll(tile[0], 64, 1), tile[1]) + bd
            hit = [
                jnp.where(number == jnp.where(left, t[0], t[1]), 1.0, 0.0) for t in (front, back)
            ]
            hits_ref[k, 0, w] = jnp.concatenate(hit, axis=0).astype(BF16)


def bias_kernel(mid_ref, wb_ref, bias_ref, w3_ref, n_ref):
    @pl.when(pl.program_id(0) == 0)
    def _():
        w = jnp.concatenate([wb_ref[...]] * 8, axis=0).T
        lane = lanes_of((128, 128))
        for k in range(8):
            hi, lo = halves(jnp.where(lane // 16 == k, w, 0.0))
            row = jnp.concatenate([hi, lo], axis=1)
            w3_ref[k] = jnp.concatenate([row, row], axis=0)

    n_ref[...] = norm(mid_ref[...])
    acc = jnp.zeros((256, 256), F32)
    for k in range(8):
        x = jnp.concatenate(
            [n_ref[pl.ds(g * 8 + k, 64, stride=32), :] for g in range(4)], axis=0
        )
        hi, lo = halves(x)
        acc = acc + mm(jnp.concatenate([hi, lo], axis=1), w3_ref[k])
    acc = acc[:, :128] + acc[:, 128:]
    for g in range(4):
        bias_ref[:, g * 128 : (g + 1) * 128] = acc[g * 64 : (g + 1) * 64]


def pick_matrix():
    row = lax.broadcasted_iota(jnp.int32, (128, 128), 0)
    return jnp.where((row // 64 == lanes_of((128, 128)) // 64) & (row % 64 == 0), 1.0, 0.0).astype(BF16)


def tokens_of(ref, n):
    x = jnp.concatenate([ref[pl.ds(q, n, stride=4), :] for q in range(3)], axis=1)
    return norm(x), ref[pl.ds(3, n, stride=4), :][:, 0:1]


def query_kernel(xr_ref, wq_ref, single_ref, wg_ref, query_ref, rowpad_ref, gate_ref):
    gate_ref[...] = 1.0 / (1.0 + jnp.exp(-mm3(norm(single_ref[...]), wg_ref[...])))
    rows, row_pad = tokens_of(xr_ref, 128)
    lane = lanes_of((16, 128))
    for m in range(4):
        a = row_pad[m * 32 : m * 32 + 16]
        b = row_pad[m * 32 + 16 : m * 32 + 32]
        rowpad_ref[m * 16 : (m + 1) * 16, :] = jnp.where(lane < 64, a, b)
    query_ref[...] = mm3(rows, wq_ref[...]) * (24.0**-0.5)


def attention_kernel(query_ref, xc_ref, bias_ref, wk_ref, wv_ref, msg_ref, colpad_ref):
    cols, col_pad = tokens_of(xc_ref, 32)
    colpad_ref[...] = jnp.broadcast_to(col_pad, (32, 128))
    query = query_ref[...]
    key = mm3(cols, wk_ref[...])
    value = mm3(cols, wv_ref[...])
    of_head = lanes_of((16, 384)) // 24 == lax.broadcasted_iota(jnp.int32, (16, 384), 0)

    def spread(y):
        return jnp.where(of_head[None], y[:, None, :], 0.0).reshape(512, 384)

    scores = mm3(query, spread(key), mm_nt) + bias_ref[...]
    of_key = lanes_of((32, 512)) // 16 == lax.broadcasted_iota(jnp.int32, (32, 512), 0)
    pad_lane = jnp.sum(jnp.where(of_key, col_pad, 0.0), axis=0, keepdims=True)
    scores = jnp.where(pad_lane > 0.5, scores, -1000000000.0)

    def over_keys(y, op):
        r = op(op(y[:, :128], y[:, 128:256]), op(y[:, 256:384], y[:, 384:]))
        for shift in (16, 32, 64):
            r = op(r, pltpu.roll(r, shift, 1))
        return r

    top = over_keys(scores, jnp.maximum)
    expo = jnp.exp(scores - jnp.concatenate([top] * 4, axis=1))
    total = over_keys(expo, jnp.add)
    acc = mm3(expo, spread(value))
    lane = lanes_of((128, 128))
    tail = jnp.where(lane < 16, total, jnp.where(lane < 32, top, 0.0))
    for q in range(3):
        msg_ref[pl.ds(q, 128, stride=4), :] = acc[:, q * 128 : (q + 1) * 128]
    msg_ref[pl.ds(3, 128, stride=4), :] = tail


def merge_kernel(msg_ref, single_ref, gate_ref, wo_ref, out_ref):
    lane = lanes_of((32, 128))
    accs, factors, totals = [], [], []
    for t in range(4):
        part = [msg_ref[pl.ds(4 * t + q, 32, stride=16), :] for q in range(4)]
        accs.append(jnp.concatenate(part[:3], axis=1))
        tail = part[3]
        local = pltpu.roll(tail, 112, 1)
        top = jnp.max(local, axis=0, keepdims=True)
        f = jnp.where(lane < 16, jnp.exp(local - top), 0.0)
        factors.append(f)
        totals.append(jnp.sum(f * tail, axis=0, keepdims=True))
    expand = jnp.where(
        lanes_of((128, 384)) // 24 == lax.broadcasted_iota(jnp.int32, (128, 384), 0), 1.0, 0.0
    )
    stacked = jnp.concatenate(factors + totals + totals, axis=0)
    wide = jnp.dot(stacked, expand, precision=lax.Precision.HIGHEST, preferred_element_type=F32)
    rows = []
    for t in range(4):
        num = jnp.sum(wide[t * 32 : (t + 1) * 32] * accs[t], axis=0, keepdims=True)
        rows.append(num / wide[128 + t : 129 + t])
    attended = jnp.concatenate(rows, axis=0)
    out_ref[...] = single_ref[...] + mm3(gate_ref[...] * attended, wo_ref[...])


def gradient_kernel(place_ref, *refs):
    parts = refs[:8]
    own_ref, hits_ref, mid_ref, rowpad_ref, colpad_ref, wdt_ref, out_ref = refs[8:15]
    f_ref, w_ref, ones_ref, pick_ref, d_ref = refs[15:]

    @pl.when(pl.program_id(0) == 0)
    def _():
        d = wdt_ref[...]
        z = jnp.zeros_like(d)
        both = jnp.concatenate(
            [jnp.concatenate([d, z], axis=1), jnp.concatenate([z, d], axis=1)], axis=0
        )
        hi, lo = halves(both)
        w_ref[0] = jnp.concatenate([hi, hi], axis=0)
        w_ref[1] = jnp.concatenate([lo, lo], axis=0)
        row = lax.broadcasted_iota(jnp.int32, (256, 128), 0) % 128
        same = row // 64 == lanes_of((256, 128)) // 64
        ones_ref[...] = jnp.where(same, 1.0, 0.0).astype(BF16)
        pick_ref[...] = pick_matrix()

    for p in range(8):
        place = place_ref[0] ^ p
        f_ref[pl.ds(pl.multiple_of(place * 64, 64), 64), :] = parts[p][pl.program_id(0)]

    lane = lanes_of((512, 128))
    first = lane < 64
    bins = lane % 64
    flip = jnp.concatenate([f_ref[pl.ds(i, 32, stride=16), :] for i in range(16)], axis=0)
    mark = jnp.where(bins == 0, flip, 0.0)
    target = mm(mark.astype(BF16), pick_ref[...])
    logits = own_ref[...].reshape(512, 128) + (flip - mark)
    top_a = jnp.max(jnp.where(first, logits, -3.0e38), axis=-1, keepdims=True)
    top_b = jnp.max(jnp.where(first, -3.0e38, logits), axis=-1, keepdims=True)
    expo = jnp.exp(logits - jnp.where(first, top_a, top_b))
    hi, lo = halves(expo)
    total = mm(jnp.concatenate([hi, lo], axis=1), ones_ref[...])
    hits = jnp.where(bins.astype(F32) == target, 1.0, 0.0) + hits_ref[...].reshape(512, 128).astype(F32)
    mask = rowpad_ref[...][:, None, :] * colpad_ref[...][None]
    hi, lo = halves(mask.reshape(512, 128) * (expo * (2.0 / total) - hits))
    d_ref[...] = jnp.concatenate([hi, lo], axis=1)
    change = mm(d_ref[...], w_ref[0]) + mm(d_ref[...], w_ref[1])
    for k in range(2):
        out_ref[0, k] = mid_ref[0, k] + change[:, k * 128 : (k + 1) * 128].reshape(16, 32, 128)


def tokens_kernel(single_ref, pad_ref, out_ref):
    tile = []
    for t in range(4):
        for q in range(3):
            tile.append(single_ref[t : t + 1, q * 128 : (q + 1) * 128])
        tile.append(jnp.full((1, 128), pad_ref[t].astype(F32)))
    out_ref[...] = jnp.broadcast_to(jnp.concatenate(tile, axis=0)[None], (32, 16, 128))


def full(shape):
    return pl.BlockSpec(shape, lambda *_: (0,) * len(shape))


def near(x):
    return pltpu.with_memory_space_constraint(x, pltpu.VMEM)


def struct(*shape):
    return jax.ShapeDtypeStruct(shape, F32)


def per_device(
    pair,
    single,
    target_bins,
    token_pad,
    w_gate,
    w_up,
    w_out,
    w_bias,
    w_query,
    w_key,
    w_value,
    w_gating,
    w_attn_out,
    w_dist,
    b_dist,
):
    at = {name: lax.axis_index(name) for name in ALL}
    coords = all_coords()
    tt = target_bins.T
    wdt = w_dist.T

    tok = pl.pallas_call(
        tokens_kernel,
        in_specs=[full((4, 384)), pl.BlockSpec(memory_space=pltpu.SMEM)],
        out_shape=struct(32, 16, 128),
        name="tokens",
    )(single, token_pad)
    rows_tok = lax.all_to_all(tok, COL, split_axis=0, concat_axis=0, tiled=True)
    rows_tok = rows_tok.reshape(512, 128)

    mid, proj, own, hits = pl.pallas_call(
        transition_kernel,
        grid=(4,),
        in_specs=[
            pl.BlockSpec((4, 2, 1, 4, 32, 128), lambda s: (0, 0, s, 0, 0, 0)),
            full((32, 128)),
            full((128, 512)),
            full((128, 512)),
            full((512, 128)),
            full((64, 128)),
            full((1, 64)),
        ],
        out_specs=[
            pl.BlockSpec((4, 2, 1, 4, 32, 128), lambda s: (0, 0, s, 0, 0, 0)),
            pl.BlockSpec((2, 1, 4, 4, 16, 128), lambda s: (0, s, 0, 0, 0, 0)),
            pl.BlockSpec((4, 1, 4, 32, 128), lambda s: (0, s, 0, 0, 0)),
            pl.BlockSpec((4, 1, 4, 32, 128), lambda s: (0, s, 0, 0, 0)),
        ],
        out_shape=[
            struct(4, 2, 4, 4, 32, 128),
            struct(2, 4, 4, 4, 16, 128),
            struct(4, 4, 4, 32, 128),
            jax.ShapeDtypeStruct((4, 4, 4, 32, 128), BF16),
        ],
        scratch_shapes=[
            pltpu.VMEM((2, 2, 256, 512), BF16),
            pltpu.VMEM((512, 256), BF16),
            pltpu.VMEM((256, 256), BF16),
        ],
        name="transition",
    )(pair.reshape(4, 2, 4, 4, 32, 128), tt, w_gate, w_up, w_out, wdt, b_dist[None])

    spread = lax.all_to_all(
        proj.reshape(32, 64, 128), PLANE, split_axis=0, concat_axis=0, tiled=True
    )
    spread = spread.reshape(8, 4, 64, 128)

    quarter = lax.dynamic_slice_in_dim(rows_tok, (at["yl"] * 2 + at["core"]) * 128, 128, 0)
    perm = [
        (flat_index(c), flat_index((c[2], c[3] ^ c[1], c[0], c[1], c[4], c[5]))) for c in coords
    ]
    cols_tok = lax.ppermute(quarter, ALL, perm)

    bias = pl.pallas_call(
        bias_kernel,
        grid=(2,),
        in_specs=[pl.BlockSpec((2048, 128), lambda m: (m, 0)), full((16, 128))],
        out_specs=pl.BlockSpec((64, 512), lambda m: (m, 0)),
        out_shape=struct(128, 512),
        scratch_shapes=[pltpu.VMEM((8, 256, 256), BF16), pltpu.VMEM((2048, 128), F32)],
        name="bias",
    )(mid.reshape(4096, 128), w_bias.T)

    query, rowpad, gate = pl.pallas_call(
        query_kernel,
        in_specs=[pl.BlockSpec(memory_space=pltpu.VMEM)] * 4,
        out_shape=[struct(128, 384), struct(64, 128), struct(4, 384)],
        name="query",
    )(near(rows_tok), w_query, single, w_gating)
    msg, colpad = pl.pallas_call(
        attention_kernel,
        in_specs=[pl.BlockSpec(memory_space=pltpu.VMEM)] * 5,
        out_shape=[struct(512, 128), struct(32, 128)],
        name="attention",
    )(query, near(cols_tok), bias, w_key, w_value)

    parts = []
    for n in range(8):
        u, v = n // 2, n % 2
        piece = lax.dynamic_index_in_dim(
            spread, (at["x"] ^ u) * 2 + (at["yh"] ^ v), 0, keepdims=False
        )
        perm = []
        for c in coords:
            x, zh, zl, yh, yl, core = c
            perm.append((flat_index(c), flat_index((zl, yh ^ v, x ^ u, zh, yl, core))))
        parts.append(lax.ppermute(piece, ALL, perm))
    place = (at["zl"] * 2 + at["zh"]).reshape(1)

    merged = lax.all_to_all(msg.reshape(32, 16, 128), COL, split_axis=0, concat_axis=0, tiled=True)
    merged = merged.reshape(512, 128)
    single_out = pl.pallas_call(
        merge_kernel,
        in_specs=[pl.BlockSpec(memory_space=pltpu.VMEM)] * 4,
        out_shape=struct(4, 384),
        name="merge",
    )(
        near(merged), single, gate, w_attn_out
    )
    grouped = pl.BlockSpec((1, 2, 16, 32, 128), lambda m, _: (m, 0, 0, 0, 0))
    pair_out = pl.pallas_call(
        gradient_kernel,
        grid_spec=pltpu.PrefetchScalarGridSpec(
            num_scalar_prefetch=1,
            grid=(4,),
            in_specs=[pl.BlockSpec(memory_space=pltpu.VMEM)] * 8
            + [
                pl.BlockSpec((16, 32, 128), lambda m, _: (m, 0, 0)),
                pl.BlockSpec((16, 32, 128), lambda m, _: (m, 0, 0)),
                grouped,
                pl.BlockSpec((16, 128), lambda m, _: (m, 0)),
                full((32, 128)),
                full((64, 128)),
            ],
            out_specs=grouped,
            scratch_shapes=[
                pltpu.VMEM((512, 128), F32),
                pltpu.VMEM((2, 256, 256), BF16),
                pltpu.VMEM((256, 128), BF16),
                pltpu.VMEM((128, 128), BF16),
                pltpu.VMEM((512, 256), BF16),
            ],
        ),
        out_shape=struct(4, 2, 16, 32, 128),
        name="gradient",
    )(
        place,
        *(near(p) for p in parts),
        own.reshape(64, 32, 128),
        hits.reshape(64, 32, 128),
        mid.reshape(4, 2, 16, 32, 128),
        rowpad,
        colpad,
        wdt,
    )
    pair_out = pair_out.reshape(128, 32, 128)
    return (pair_out, single_out)


def solution(mesh):
    fine = Mesh(mesh.devices.reshape(SIZES), ALL)
    row, col = ("x", "zh"), COL
    in_specs = (
        P(row, col, None),
        P(ALL, None),
        P(row, col),
        P(ALL),
    ) + (P(),) * 11
    out_specs = (P(row, col, None), P(ALL, None))
    return jax.shard_map(
        per_device, mesh=fine, in_specs=in_specs, out_specs=out_specs, check_vma=False
    )
```
